256 devices in a mesh: dp: 8 (over z), seq: 32 (over x, y, core).
Axes of the slice: x: 4, y: 4, z: 8, core: 2. Of those that a mesh axis runs over, the one named last changes fastest.
Arguments:
- tokens: bfloat16 [8, 16384, 256], P('dp', 'seq'), may hold values from -6 to 6
- cotangent: bfloat16 [8, 16384, 256], P('dp', 'seq'), may hold values from -6 to 6
- w_in: bfloat16 [256, 768], replicated, may hold values from -0.375 to 0.375
- w_out: bfloat16 [256, 256], replicated, may hold values from -0.375 to 0.375
- filter_taps: float32 [16384, 256], P('seq'), may hold values from -0.046875 to 0.046875
- skip: float32 [256], replicated, may hold values from -4 to 4
Outputs:
- output: bfloat16 [8, 16384, 256], P('dp', 'seq')
- dinput: bfloat16 [8, 16384, 256], P('dp', 'seq')
- grad_in_proj: float32 [256, 768], P('dp')
- grad_out_proj: float32 [256, 256], P('dp')
- grad_filter: float32 [16384, 256], P('seq', 'dp')
- grad_skip: float32 [256], P('dp')
The draws below stay inside these ranges and needn't reach their ends.
All inputs are finite; a program needn't handle non-finite values.
Results may differ from the reference program's by a relative error of at most 0.0049.
Values sent between devices are 32-bit elements; how exact they have to be, the bound alone decides.
A program may use at most 128 MiB of HBM per device.

```python
import math
import jax
import jax.numpy as jnp
from jax import lax

D = 256
SEQS = 8
LENGTH = 16384


def shard_levels(key, shape, pieces, least, top_value):
    factor_of, own = 1.0, jax.random.fold_in(key, 6)
    for dim, blocks in pieces:
        steps = jnp.exp(jax.random.uniform(jax.random.fold_in(own, dim), (blocks,), jnp.float32, least / len(pieces), top_value / len(pieces)))
        factor_of = factor_of * jnp.repeat(steps, shape[dim] // blocks).reshape([-1 if axis == dim else 1 for axis in range(len(shape))])
    return factor_of


def centred(stream_key, shape, deviation, bound, split=(), held_as=jnp.bfloat16):
    factor_of = shard_levels(stream_key, shape, split, -0.22, 0.18) if split else 1.0
    drawn = jax.random.normal(stream_key, shape, jnp.float32) * deviation * factor_of
    return jnp.minimum(jnp.maximum(drawn, -bound), bound).astype(held_as)


def setup_inputs(seed: int = 0) -> dict:
    streams_of = jax.random.split(jax.random.key(seed), 7)
    return {
        "tokens": centred(streams_of[0], (SEQS, LENGTH, D), 1.0, 6.0, ((0, 8), (1, 32))),
        "cotangent": centred(streams_of[1], (SEQS, LENGTH, D), 1.0, 6.0, ((0, 8), (1, 32))),
        "w_in": centred(streams_of[2], (D, 3 * D), D ** -0.5, 0.375),
        "w_out": centred(streams_of[3], (D, D), D ** -0.5, 0.375),
        "filter_taps": centred(streams_of[4], (LENGTH, D), LENGTH ** -0.5, 0.046875, ((0, 32),), jnp.float32),
        "skip": centred(streams_of[5], (D,), 1.0, 4.0, (), jnp.float32),
    }


def reference(tokens, cotangent, w_in, w_out, filter_taps, skip):
    model_width = w_out.shape[0]
    seq_length = tokens.shape[1]
    padded = 2 * seq_length
    taps_spec = jnp.fft.rfft(filter_taps, n=padded, axis=0)

    def one_sequence(carry, pair):
        seq_in, grad_out = pair
        projected = jnp.dot(seq_in, w_in, preferred_element_type=jnp.float32)
        gate_out = projected[:, :model_width]
        gate_in = projected[:, model_width:2 * model_width]
        values = projected[:, 2 * model_width:]
        gated = values * gate_in
        gated_spec = jnp.fft.rfft(gated, n=padded, axis=0)
        conv = jnp.fft.irfft(gated_spec * taps_spec, n=padded, axis=0)[:seq_length] + skip * gated
        mixed = (conv * gate_out).astype(jnp.bfloat16)
        output = jnp.dot(mixed, w_out, preferred_element_type=jnp.float32).astype(jnp.bfloat16)
        dmixed = jnp.dot(grad_out, w_out.T, preferred_element_type=jnp.float32)
        dconv = dmixed * gate_out
        dconv_spec = jnp.fft.rfft(dconv, n=padded, axis=0)
        dgated = jnp.fft.irfft(jnp.conj(taps_spec) * dconv_spec, n=padded, axis=0)[:seq_length] + skip * dconv
        taps_term = jnp.fft.irfft(jnp.conj(gated_spec) * dconv_spec, n=padded, axis=0)[:seq_length]
        dproj = jnp.concatenate([dmixed * conv, dgated * values, dgated * gate_in], axis=1).astype(jnp.bfloat16)
        dinput = jnp.dot(dproj, w_in.T, preferred_element_type=jnp.float32).astype(jnp.bfloat16)
        in_term = jnp.dot(seq_in.T, dproj, preferred_element_type=jnp.float32)
        out_term = jnp.dot(mixed.T, grad_out, preferred_element_type=jnp.float32)
        skip_term = lax.optimization_barrier(jnp.sum(dconv * gated, axis=0))
        in_acc, out_acc, taps_acc, skip_acc = carry
        return ((in_acc + in_term, out_acc + out_term, taps_acc + taps_term, skip_acc + skip_term), (output, dinput))
    start = (jnp.zeros((model_width, 3 * model_width), jnp.float32), jnp.zeros((model_width, model_width), jnp.float32), jnp.zeros((seq_length, model_width), jnp.float32), jnp.zeros((model_width,), jnp.float32))
    totals, stacked = lax.scan(one_sequence, start, (tokens, cotangent))
    grad_scale = 1.0 / math.sqrt(tokens.shape[0] * seq_length)
    return (stacked[0], stacked[1], totals[0] * grad_scale, totals[1] * grad_scale, totals[2] * grad_scale, totals[3] * grad_scale)
```

```python
import functools
import math

import jax
import jax.numpy as jnp
import numpy as np
from jax import lax
from jax.experimental import pallas as pl
from jax.experimental.pallas import tpu as pltpu
from jax.sharding import PartitionSpec as P

F32 = jnp.float32
BF16 = jnp.bfloat16
ROWS = 16
NT = (((1,), (1,)), ((), ()))
TN = (((0,), (0,)), ((), ()))


def tables(block):
    def turn(numer):
        angle = np.pi / (2 * block) * (numer % (4 * block))
        return np.cos(angle), np.sin(angle)

    pos = np.arange(block)
    coarse = np.arange(block // ROWS) * ROWS
    fine = np.arange(ROWS)
    odd = 2 * pos + 1
    parts = [
        *turn(np.outer(coarse, odd)),
        *turn(np.outer(fine, odd)),
        *turn(np.outer(2 * coarse, pos)),
        *turn(np.outer(2 * fine + 1, pos)),
    ]
    return np.concatenate(parts, axis=0).astype(np.float32)


def split2(x):
    high = x.astype(BF16)
    return high, (x - high.astype(F32)).astype(BF16)


def split3(x):
    high = x.astype(BF16)
    rest = x - high.astype(F32)
    mid = rest.astype(BF16)
    return high, mid, (rest - mid.astype(F32)).astype(BF16)


def dot(a, b, dims=(((1,), (0,)), ((), ()))):
    return lax.dot_general(a, b, dims, preferred_element_type=F32)


def block_conv(p_ref, q_ref, o_ref, block, size, corr):
    count = q_ref.shape[0]
    groups = count // size
    lanes = min(128, block)

    def tile(t, _):
        re = pl.ds(pl.multiple_of(t * lanes, lanes), lanes)
        im = pl.ds(pl.multiple_of(block + t * lanes, lanes), lanes)

        def chunk(acc, out0, in0, diag):
            acc = list(acc)
            cache = {}
            base = in0 - out0 if corr else out0 - in0
            for u in range(size):
                qr, qi = q_ref[in0 + u, :, re], q_ref[in0 + u, :, im]
                for r in range(size):
                    lag = u - r if corr else r - u
                    if diag and lag < 0:
                        continue
                    if lag not in cache:
                        cache[lag] = p_ref[base + lag, :, re], p_ref[base + lag, :, im]
                    pr, pi = cache[lag]
                    if corr:
                        new_re, new_im = pr * qr + pi * qi, pr * qi - pi * qr
                    else:
                        new_re, new_im = pr * qr - pi * qi, pr * qi + pi * qr
                    acc[2 * r] = acc[2 * r] + new_re
                    acc[2 * r + 1] = acc[2 * r + 1] + new_im
            return tuple(acc)

        def group(g, _):
            out0 = g * size
            zero = jnp.zeros((q_ref.shape[1], lanes), F32)
            acc = chunk((zero,) * (2 * size), out0, out0, True)

            def step(h, acc):
                return chunk(acc, out0, h * size, False)

            low, top = (g + 1, groups) if corr else (0, g)
            acc = lax.fori_loop(low, top, step, acc)
            for r in range(size):
                o_ref[out0 + r, :, re] = acc[2 * r]
                o_ref[out0 + r, :, im] = acc[2 * r + 1]
            return 0

        lax.fori_loop(0, groups, group, 0)
        return 0

    lax.fori_loop(0, block // lanes, tile, 0)


def body(
    seq_n,
    dp_n,
    scale,
    tok,
    cot,
    w_in,
    w_out,
    taps,
    skip,
    tab,
    out,
    dinp,
    gin,
    gout,
    gfil,
    gskip,
    tap_s,
    gat_s,
    dcn_s,
    tap_r,
    gat_r,
    dcn_r,
    proj,
    dmx,
    w_t,
    w_o,
    tok_t,
    f_mat,
    b_mat,
    h_sp,
    x_sp,
    d_sp,
    o_sp,
    con_s,
    dga_s,
    con_r,
    dga_r,
    gf_t,
    gf_s,
    gf_r,
    sk_s,
    sk_r,
    q_s,
    q_r,
    dproj,
    g1_s,
    g2_s,
    g1_r,
    g2_r,
    z_s,
    z_r,
    a_s,
    a_r,
    send,
    recv,
):
    block, width = tok.shape
    chans = width // seq_n
    me = lax.axis_index("seq")
    my_dp = lax.axis_index("dp")
    group = 8 if seq_n >= 32 else 4

    barrier = pltpu.get_barrier_semaphore()

    def greet_seq(k, _):
        pl.semaphore_signal(barrier, 1, device_id={"seq": lax.rem(me + k, seq_n)})
        return 0

    def greet_dp(k, _):
        pl.semaphore_signal(barrier, 1, device_id={"dp": lax.rem(my_dp + k, dp_n)})
        return 0

    lax.fori_loop(1, seq_n, greet_seq, 0)
    lax.fori_loop(1, dp_n, greet_dp, 0)

    def exchange(src, dst, slot, axis="seq", gather=False):
        mine, parts = (me, seq_n) if axis == "seq" else (my_dp, dp_n)
        own = src if gather else src.at[mine]
        pltpu.make_async_copy(own, dst.at[mine], recv.at[slot]).start()

        def go(k, _):
            peer = lax.rem(mine + k, parts)
            pltpu.make_async_remote_copy(
                src if gather else src.at[peer],
                dst.at[mine],
                send.at[slot],
                recv.at[slot],
                device_id={axis: peer},
            ).start()
            return 0

        lax.fori_loop(1, parts, go, 0)

    def arrived(dst, slot):
        pltpu.make_async_copy(dst, dst, recv.at[slot]).wait()

    def sent(dst, slot):
        rest = dst.at[pl.ds(0, dst.shape[0] - 1)]
        pltpu.make_async_copy(rest, rest, send.at[slot]).wait()

    row = lax.broadcasted_iota(jnp.int32, (width, width), 0)
    col = lax.broadcasted_iota(jnp.int32, (width, width), 1)
    hit = (col % seq_n) * chans + col // seq_n == row
    perm = jnp.where(hit, 1.0, 0.0).astype(BF16)
    skip_col = jnp.sum(jnp.where(hit, skip[...], 0.0), axis=1, keepdims=True)

    high, low = split2(taps[...])
    taps_t = dot(perm, high, NT) + dot(perm, low, NT)
    tap_s[...] = taps_t.reshape(seq_n, chans, block)
    pl.semaphore_wait(barrier, seq_n + dp_n - 2)
    exchange(tap_s, tap_r, 0)

    for part in range(3):
        rows = pl.ds(part * width, width)
        w_t[rows, :] = dot(perm, w_in[:, part * width : (part + 1) * width], NT).astype(BF16)
        proj[rows, :] = dot(w_t[rows, :], tok[...], NT)
    gate_out = proj.at[pl.ds(0, width)]
    gate_in = proj.at[pl.ds(width, width)]
    values = proj.at[pl.ds(2 * width, width)]
    gat_s[...] = (values[...] * gate_in[...]).reshape(seq_n, chans, block)
    exchange(gat_s, gat_r, 1)

    w_o[...] = dot(perm, w_out[...]).astype(BF16)
    dmx[...] = dot(w_o[...], cot[...], NT)
    dcn_s[...] = (dmx[...] * gate_out[...]).reshape(seq_n, chans, block)
    exchange(dcn_s, dcn_r, 2)
    tok_t[...] = dot(perm, tok[...], NT).astype(BF16)

    big = block // ROWS

    def build(dst, first, vertical):
        cos_f = tab[pl.ds(first + 2 * big, ROWS), :]
        sin_f = tab[pl.ds(first + 2 * big + ROWS, ROWS), :]

        def rows_of(a, _):
            cos_c = tab[pl.ds(first + a, 1), :]
            sin_c = tab[pl.ds(first + big + a, 1), :]
            cos = cos_c * cos_f - sin_c * sin_f
            sin = -(sin_c * cos_f + cos_c * sin_f)
            at = pl.multiple_of(a * ROWS, ROWS)
            for k, value in enumerate((cos, sin)):
                high, low = split2(value)
                for copy, piece in enumerate((high, high, low)):
                    if vertical:
                        dst[pl.ds((2 * copy + k) * block + at, ROWS), :] = piece
                    else:
                        dst[pl.ds(copy * block + at, ROWS), k * block : (k + 1) * block] = piece
            return 0

        lax.fori_loop(0, big, rows_of, 0)

    build(f_mat, 0, False)
    build(b_mat, 2 * big + 2 * ROWS, True)

    rows_n = seq_n * chans
    step = min(256, block)

    def spectrum(src, dst):
        high, low = split2(src[...].reshape(rows_n, block))
        wide = jnp.concatenate([high, low, high], axis=1)
        for n in range(0, 2 * block, step):
            dst[:, :, n : n + step] = dot(wide, f_mat[:, n : n + step]).reshape(seq_n, chans, step)

    def field(factor):
        high, low = split2(o_sp[...].reshape(rows_n, 2 * block))
        wide = jnp.concatenate([high, low, high], axis=1)
        return dot(wide, b_mat[...]) * factor

    odd = lax.broadcasted_iota(jnp.int32, (1, 1, block), 2) % 2
    sign = (1 - 2 * odd).astype(F32)

    arrived(tap_r, 0)
    spectrum(tap_r, o_sp)
    h_sp[0] = o_sp[0]
    h_sp[1:, :, :block] = o_sp[1:, :, :block] - sign * o_sp[: seq_n - 1, :, block:]
    h_sp[1:, :, block:] = o_sp[1:, :, block:] + sign * o_sp[: seq_n - 1, :, :block]

    arrived(gat_r, 1)
    spectrum(gat_r, x_sp)
    block_conv(h_sp, x_sp, o_sp, block, group, False)
    con_s[...] = field(1.0 / block).reshape(seq_n, chans, block)
    exchange(con_s, con_r, 3)

    arrived(dcn_r, 2)
    spectrum(dcn_r, d_sp)
    block_conv(h_sp, d_sp, o_sp, block, group, True)
    dga_s[...] = field(1.0 / block).reshape(seq_n, chans, block)
    exchange(dga_s, dga_r, 4)

    block_conv(x_sp, d_sp, h_sp, block, group, True)
    last = seq_n - 1
    o_sp[last] = h_sp[last]
    o_sp[:last, :, :block] = h_sp[:last, :, :block] + sign * h_sp[1:, :, block:]
    o_sp[:last, :, block:] = h_sp[:last, :, block:] - sign * h_sp[1:, :, :block]
    lanes = block // 4
    term = field(scale / block)
    for r in range(4):
        gf_t[r] = term[:, r * lanes : (r + 1) * lanes]
        for d in range(dp_n):
            gf_s[d, :, r * lanes : (r + 1) * lanes] = gf_t[r, pl.ds(d, seq_n, stride=chans), :]
    both = jnp.sum(gat_r[...] * dcn_r[...], axis=0)
    narrow = both[:, :lanes]
    for r in range(1, 4):
        narrow = narrow + both[:, r * lanes : (r + 1) * lanes]
    for d in range(dp_n):
        sk_s[d] = jnp.broadcast_to(narrow[d : d + 1, :], (8, lanes))
    exchange(gf_s, gf_r, 5, "dp")
    exchange(sk_s, sk_r, 6, "dp")

    arrived(con_r, 3)
    gated = gat_s[...].reshape(width, block)
    conv = con_r[...].reshape(width, block) + skip_col * gated
    mixed = (conv * gate_out[...]).astype(BF16)
    dproj[pl.ds(0, width), :] = (dmx[...] * conv).astype(BF16)
    g1_s[:, :, :width] = dot(tok_t[...], dproj[pl.ds(0, width), :], NT).reshape(seq_n, chans, width)
    g1_s[:, :, width:] = dot(mixed, cot[...]).reshape(seq_n, chans, width)
    exchange(g1_s, g1_r, 7)
    out[...] = dot(mixed, w_o[...], TN).astype(BF16)

    arrived(gf_r, 5)
    arrived(sk_r, 6)
    gf_sum = jnp.sum(gf_r[...], axis=0)
    sk_sum = jnp.sum(sk_r[...], axis=0) * scale
    for r in range(4):
        q_s[:, r, :] = gf_sum[:, r * lanes : (r + 1) * lanes]
    q_s[:, 4, :] = jnp.broadcast_to(sk_sum[0:1, :], (seq_n, lanes))
    exchange(q_s, q_r, 8)

    arrived(dga_r, 4)
    dgated = dga_r[...].reshape(width, block) + skip_col * dcn_s[...].reshape(width, block)
    dproj[pl.ds(width, width), :] = (dgated * values[...]).astype(BF16)
    dproj[pl.ds(2 * width, width), :] = (dgated * gate_in[...]).astype(BF16)
    for k in (0, 1):
        term = dot(tok_t[...], dproj[pl.ds((k + 1) * width, width), :], NT)
        g2_s[:, :, k * width : (k + 1) * width] = term.reshape(seq_n, chans, width)
    exchange(g2_s, g2_r, 9)
    dinp[...] = dot(dproj[...], w_t[...], TN).astype(BF16)

    arrived(q_r, 8)
    for r in range(4):
        gfil[r * lanes : (r + 1) * lanes, :] = q_r[:, r, :].T
    gskip[...] = jnp.sum(q_r[:, 4, :].T, axis=0, keepdims=True)

    arrived(g1_r, 7)
    sum1 = jnp.sum(g1_r[...], axis=0) * scale
    arrived(g2_r, 9)
    sum2 = jnp.sum(g2_r[...], axis=0) * scale
    piece = 2 * width // 4
    for r in range(4):
        z_s[:, r, :] = sum1[:, r * piece : (r + 1) * piece]
        z_s[:, 4 + r, :] = sum2[:, r * piece : (r + 1) * piece]
    exchange(z_s, z_r, 10, "dp")
    arrived(z_r, 10)
    a_s[...] = jnp.sum(z_r[...], axis=0)
    exchange(a_s, a_r, 11, gather=True)
    arrived(a_r, 11)

    def line(r):
        return jnp.concatenate([a_r[:, r, :], a_r[:, r + 1, :]], axis=1)

    gout[...] = line(2)
    for k, r in enumerate((0, 4, 6)):
        h, m, t = split3(line(r))
        gin[:, k * width : (k + 1) * width] = dot(h, perm) + (dot(m, perm) + dot(t, perm))

    for slot, ref in enumerate(
        (tap_r, gat_r, dcn_r, con_r, dga_r, gf_r, sk_r, g1_r, q_r, g2_r, z_r, a_r)
    ):
        sent(ref, slot)


def shards(tokens, cotangent, w_in, w_out, filter_taps, skip):
    seq_n, dp_n = lax.axis_size("seq"), lax.axis_size("dp")
    block, width = tokens.shape[1:]
    chans = width // seq_n
    scale = 1.0 / math.sqrt(dp_n * seq_n * block)
    own = width // dp_n

    def shape(*dims, dtype=F32):
        return pltpu.VMEM(dims, dtype)

    ex = (seq_n, chans, block)
    sp = (seq_n, chans, 2 * block)
    scratch = [
        *[shape(*ex)] * 6,
        shape(3 * width, block),
        shape(width, block),
        shape(3 * width, width, dtype=BF16),
        shape(width, width, dtype=BF16),
        shape(width, block, dtype=BF16),
        shape(3 * block, 2 * block, dtype=BF16),
        shape(6 * block, block, dtype=BF16),
        *[shape(*sp)] * 4,
        *[shape(*ex)] * 4,
        shape(4, width, block // 4),
        *[shape(dp_n, seq_n, block)] * 2,
        *[shape(dp_n, 8, block // 4)] * 2,
        *[shape(seq_n, 8, block // 4)] * 2,
        shape(3 * width, block, dtype=BF16),
        *[shape(seq_n, chans, 2 * width)] * 4,
        *[shape(dp_n, 8, width // 2)] * 2,
        shape(8, width // 2),
        shape(seq_n, 8, width // 2),
        pltpu.SemaphoreType.DMA((12,)),
        pltpu.SemaphoreType.DMA((12,)),
    ]
    vmem = pl.BlockSpec(memory_space=pltpu.VMEM)
    out, dinp, gin, gout, gfil, gskip = pl.pallas_call(
        functools.partial(body, seq_n, dp_n, scale),
        out_shape=(
            jax.ShapeDtypeStruct((block, width), BF16),
            jax.ShapeDtypeStruct((block, width), BF16),
            jax.ShapeDtypeStruct((own, 3 * width), F32),
            jax.ShapeDtypeStruct((own, width), F32),
            jax.ShapeDtypeStruct((block, own), F32),
            jax.ShapeDtypeStruct((1, own), F32),
        ),
        in_specs=[vmem] * 7,
        out_specs=(vmem,) * 6,
        scratch_shapes=scratch,
        compiler_params=pltpu.CompilerParams(
            collective_id=0, has_side_effects=True, vmem_limit_bytes=56 * 1024 * 1024
        ),
        name="operator",
    )(tokens[0], cotangent[0], w_in, w_out, filter_taps, skip[None], jnp.asarray(tables(block)))
    return out[None], dinp[None], gin, gout, gfil, gskip[0]


def solution(mesh):
    return jax.shard_map(
        shards,
        mesh=mesh,
        in_specs=(P("dp", "seq", None), P("dp", "seq", None), P(), P(), P("seq", None), P()),
        out_specs=(
            P("dp", "seq", None),
            P("dp", "seq", None),
            P("dp", None),
            P("dp", None),
            P("seq", "dp"),
            P("dp"),
        ),
        check_vma=False,
    )
```

```python
import functools
import math

import jax
import jax.numpy as jnp
import numpy as np
from jax import lax
from jax.experimental import pallas as pl
from jax.experimental.pallas import tpu as pltpu
from jax.sharding import PartitionSpec as P

F32 = jnp.float32
BF16 = jnp.bfloat16
ROWS = 16
NT = (((1,), (1,)), ((), ()))
TN = (((0,), (0,)), ((), ()))


def tables(block):
    def turn(numer):
        angle = np.pi / (2 * block) * (numer % (4 * block))
        return np.cos(angle), np.sin(angle)

    pos = np.arange(block)
    coarse = np.arange(block // ROWS) * ROWS
    fine = np.arange(ROWS)
    odd = 2 * pos + 1
    parts = [
        *turn(np.outer(coarse, odd)),
        *turn(np.outer(fine, odd)),
        *turn(np.outer(2 * coarse, pos)),
        *turn(np.outer(2 * fine + 1, pos)),
    ]
    return np.concatenate(parts, axis=0).astype(np.float32)


def split2(x):
    high = x.astype(BF16)
    return high, (x - high.astype(F32)).astype(BF16)


def split3(x):
    high = x.astype(BF16)
    rest = x - high.astype(F32)
    mid = rest.astype(BF16)
    return high, mid, (rest - mid.astype(F32)).astype(BF16)


def dot(a, b, dims=(((1,), (0,)), ((), ()))):
    return lax.dot_general(a, b, dims, preferred_element_type=F32)


def block_conv(p_ref, q_ref, o_ref, block, size, corr):
    count = q_ref.shape[0]
    groups = count // size
    lanes = min(128, block)

    def tile(t, _):
        re = pl.ds(pl.multiple_of(t * lanes, lanes), lanes)
        im = pl.ds(pl.multiple_of(block + t * lanes, lanes), lanes)

        def chunk(acc, out0, in0, diag):
            acc = list(acc)
            cache = {}
            base = in0 - out0 if corr else out0 - in0
            for u in range(size):
                qr, qi = q_ref[in0 + u, :, re], q_ref[in0 + u, :, im]
                for r in range(size):
                    lag = u - r if corr else r - u
                    if diag and lag < 0:
                        continue
                    if lag not in cache:
                        cache[lag] = p_ref[base + lag, :, re], p_ref[base + lag, :, im]
                    pr, pi = cache[lag]
                    if corr:
                        new_re, new_im = pr * qr + pi * qi, pr * qi - pi * qr
                    else:
                        new_re, new_im = pr * qr - pi * qi, pr * qi + pi * qr
                    acc[2 * r] = acc[2 * r] + new_re
                    acc[2 * r + 1] = acc[2 * r + 1] + new_im
            return tuple(acc)

        def group(g, _):
            out0 = g * size
            zero = jnp.zeros((q_ref.shape[1], lanes), F32)
            acc = chunk((zero,) * (2 * size), out0, out0, True)

            def step(h, acc):
                return chunk(acc, out0, h * size, False)

            low, top = (g + 1, groups) if corr else (0, g)
            acc = lax.fori_loop(low, top, step, acc)
            for r in range(size):
                o_ref[out0 + r, :, re] = acc[2 * r]
                o_ref[out0 + r, :, im] = acc[2 * r + 1]
            return 0

        lax.fori_loop(0, groups, group, 0)
        return 0

    lax.fori_loop(0, block // lanes, tile, 0)


def body(
    seq_n,
    dp_n,
    scale,
    tok,
    cot,
    w_in,
    w_out,
    taps,
    skip,
    tab,
    out,
    dinp,
    gin,
    gout,
    gfil,
    gskip,
    tap_s,
    gat_s,
    dcn_s,
    tap_r,
    gat_r,
    dcn_r,
    proj,
    dmx,
    w_t,
    w_o,
    tok_t,
    f_mat,
    b_mat,
    h_sp,
    x_sp,
    d_sp,
    o_sp,
    con_s,
    dga_s,
    con_r,
    dga_r,
    gf_t,
    gf_s,
    gf_r,
    sk_s,
    sk_r,
    q_s,
    q_r,
    dproj,
    g1_s,
    g2_s,
    p1_r,
    p2_r,
    r1_s,
    r2_s,
    r1_r,
    r2_r,
    z_s,
    z_r,
    a_s,
    a_r,
    send,
    recv,
):
    block, width = tok.shape
    chans = width // seq_n
    me = lax.axis_index("seq")
    my_dp = lax.axis_index("dp")
    core = lax.rem(me, 2)
    group = 8 if seq_n >= 32 else 4

    barrier = pltpu.get_barrier_semaphore()

    def greet_seq(k, _):
        pl.semaphore_signal(barrier, 1, device_id={"seq": lax.rem(me + k, seq_n)})
        return 0

    def greet_dp(k, _):
        pl.semaphore_signal(barrier, 1, device_id={"dp": lax.rem(my_dp + k, dp_n)})
        return 0

    lax.fori_loop(1, seq_n, greet_seq, 0)
    lax.fori_loop(1, dp_n, greet_dp, 0)

    def exchange(src, dst, slot, axis="seq", gather=False, cores=1):
        mine, parts = (me // cores, seq_n // cores) if axis == "seq" else (my_dp, dp_n)
        own = src if gather else src.at[mine]
        pltpu.make_async_copy(own, dst.at[mine], recv.at[slot]).start()

        def go(k, _):
            peer = lax.rem(mine + k, parts)
            pltpu.make_async_remote_copy(
                src if gather else src.at[peer],
                dst.at[mine],
                send.at[slot],
                recv.at[slot],
                device_id={axis: peer if cores == 1 else peer * cores + core},
            ).start()
            return 0

        lax.fori_loop(1, parts, go, 0)

    def swap(src, dst, slot):
        pltpu.make_async_remote_copy(
            src.at[1 - core],
            dst,
            send.at[slot],
            recv.at[slot],
            device_id={"seq": me + 1 - 2 * core},
        ).start()

    def arrived(dst, slot):
        pltpu.make_async_copy(dst, dst, recv.at[slot]).wait()

    def sent(dst, slot):
        rest = dst.at[pl.ds(0, dst.shape[0] - 1)]
        pltpu.make_async_copy(rest, rest, send.at[slot]).wait()

    row = lax.broadcasted_iota(jnp.int32, (width, width), 0)
    col = lax.broadcasted_iota(jnp.int32, (width, width), 1)
    hit = (col % seq_n) * chans + col // seq_n == row
    perm = jnp.where(hit, 1.0, 0.0).astype(BF16)
    skip_col = jnp.sum(jnp.where(hit, skip[...], 0.0), axis=1, keepdims=True)

    high, low = split2(taps[...])
    taps_t = dot(perm, high, NT) + dot(perm, low, NT)
    tap_s[...] = taps_t.reshape(seq_n, chans, block)

    for part in range(3):
        rows = pl.ds(part * width, width)
        w_t[rows, :] = dot(perm, w_in[:, part * width : (part + 1) * width], NT).astype(BF16)
        proj[rows, :] = dot(w_t[rows, :], tok[...], NT)
    gate_out = proj.at[pl.ds(0, width)]
    gate_in = proj.at[pl.ds(width, width)]
    values = proj.at[pl.ds(2 * width, width)]
    gat_s[...] = (values[...] * gate_in[...]).reshape(seq_n, chans, block)

    w_o[...] = dot(perm, w_out[...]).astype(BF16)
    dmx[...] = dot(w_o[...], cot[...], NT)
    dcn_s[...] = (dmx[...] * gate_out[...]).reshape(seq_n, chans, block)
    pl.semaphore_wait(barrier, seq_n + dp_n - 2)
    exchange(tap_s, tap_r, 0)
    exchange(gat_s, gat_r, 1)
    exchange(dcn_s, dcn_r, 2)
    tok_t[...] = dot(perm, tok[...], NT).astype(BF16)

    big = block // ROWS

    def build(dst, first, vertical):
        cos_f = tab[pl.ds(first + 2 * big, ROWS), :]
        sin_f = tab[pl.ds(first + 2 * big + ROWS, ROWS), :]

        def rows_of(a, _):
            cos_c = tab[pl.ds(first + a, 1), :]
            sin_c = tab[pl.ds(first + big + a, 1), :]
            cos = cos_c * cos_f - sin_c * sin_f
            sin = -(sin_c * cos_f + cos_c * sin_f)
            at = pl.multiple_of(a * ROWS, ROWS)
            for k, value in enumerate((cos, sin)):
                high, low = split2(value)
                for copy, piece in enumerate((high, high, low)):
                    if vertical:
                        dst[pl.ds((2 * copy + k) * block + at, ROWS), :] = piece
                    else:
                        dst[pl.ds(copy * block + at, ROWS), k * block : (k + 1) * block] = piece
            return 0

        lax.fori_loop(0, big, rows_of, 0)

    build(f_mat, 0, False)
    build(b_mat, 2 * big + 2 * ROWS, True)

    rows_n = seq_n * chans
    step = min(256, block)

    def spectrum(src, dst):
        high, low = split2(src[...].reshape(rows_n, block))
        wide = jnp.concatenate([high, low, high], axis=1)
        for n in range(0, 2 * block, step):
            dst[:, :, n : n + step] = dot(wide, f_mat[:, n : n + step]).reshape(seq_n, chans, step)

    def field(factor):
        high, low = split2(o_sp[...].reshape(rows_n, 2 * block))
        wide = jnp.concatenate([high, low, high], axis=1)
        return dot(wide, b_mat[...]) * factor

    odd = lax.broadcasted_iota(jnp.int32, (1, 1, block), 2) % 2
    sign = (1 - 2 * odd).astype(F32)

    arrived(tap_r, 0)
    spectrum(tap_r, o_sp)
    h_sp[0] = o_sp[0]
    h_sp[1:, :, :block] = o_sp[1:, :, :block] - sign * o_sp[: seq_n - 1, :, block:]
    h_sp[1:, :, block:] = o_sp[1:, :, block:] + sign * o_sp[: seq_n - 1, :, :block]

    arrived(gat_r, 1)
    spectrum(gat_r, x_sp)
    block_conv(h_sp, x_sp, o_sp, block, group, False)
    con_s[...] = field(1.0 / block).reshape(seq_n, chans, block)
    exchange(con_s, con_r, 3)

    arrived(dcn_r, 2)
    spectrum(dcn_r, d_sp)
    block_conv(h_sp, d_sp, o_sp, block, group, True)
    dga_s[...] = field(1.0 / block).reshape(seq_n, chans, block)
    exchange(dga_s, dga_r, 4)

    block_conv(x_sp, d_sp, h_sp, block, group, True)
    last = seq_n - 1
    o_sp[last] = h_sp[last]
    o_sp[:last, :, :block] = h_sp[:last, :, :block] + sign * h_sp[1:, :, block:]
    o_sp[:last, :, block:] = h_sp[:last, :, block:] - sign * h_sp[1:, :, :block]
    lanes = block // 4
    term = field(scale / block)
    for r in range(4):
        gf_t[r] = term[:, r * lanes : (r + 1) * lanes]
        for d in range(dp_n):
            gf_s[d, :, r * lanes : (r + 1) * lanes] = gf_t[r, pl.ds(d, seq_n, stride=chans), :]
    both = jnp.sum(gat_r[...] * dcn_r[...], axis=0)
    narrow = both[:, :lanes]
    for r in range(1, 4):
        narrow = narrow + both[:, r * lanes : (r + 1) * lanes]
    for d in range(dp_n):
        sk_s[d] = jnp.broadcast_to(narrow[d : d + 1, :], (8, lanes))
    exchange(gf_s, gf_r, 5, "dp")
    exchange(sk_s, sk_r, 6, "dp")

    arrived(con_r, 3)
    gated = gat_s[...].reshape(width, block)
    conv = con_r[...].reshape(width, block) + skip_col * gated
    mixed = (conv * gate_out[...]).astype(BF16)
    dproj[pl.ds(0, width), :] = (dmx[...] * conv).astype(BF16)

    def fill(dst, first, term):
        term = term.reshape(seq_n // 2, 2, chans, width)
        for c in (0, 1):
            dst[c, :, :, first : first + width] = term[:, c]

    fill(g1_s, 0, dot(tok_t[...], dproj[pl.ds(0, width), :], NT))
    fill(g1_s, width, dot(mixed, cot[...]))
    swap(g1_s, p1_r, 7)
    out[...] = dot(mixed, w_o[...], TN).astype(BF16)
    arrived(p1_r, 7)
    r1_s[...] = g1_s[core] + p1_r[...]
    exchange(r1_s, r1_r, 12, cores=2)

    arrived(dga_r, 4)
    dgated = dga_r[...].reshape(width, block) + skip_col * dcn_s[...].reshape(width, block)
    dproj[pl.ds(width, width), :] = (dgated * values[...]).astype(BF16)
    dproj[pl.ds(2 * width, width), :] = (dgated * gate_in[...]).astype(BF16)
    for k in (0, 1):
        fill(g2_s, k * width, dot(tok_t[...], dproj[pl.ds((k + 1) * width, width), :], NT))
    swap(g2_s, p2_r, 9)
    arrived(p2_r, 9)
    r2_s[...] = g2_s[core] + p2_r[...]
    exchange(r2_s, r2_r, 13, cores=2)
    dinp[...] = dot(dproj[...], w_t[...], TN).astype(BF16)

    arrived(gf_r, 5)
    arrived(sk_r, 6)
    gf_sum = jnp.sum(gf_r[...], axis=0)
    sk_sum = jnp.sum(sk_r[...], axis=0) * scale
    for r in range(4):
        q_s[:, r, :] = gf_sum[:, r * lanes : (r + 1) * lanes]
    q_s[:, 4, :] = jnp.broadcast_to(sk_sum[0:1, :], (seq_n, lanes))
    exchange(q_s, q_r, 8)

    arrived(r1_r, 12)
    sum1 = jnp.sum(r1_r[...], axis=0) * scale
    piece = 2 * width // 4
    for r in range(4):
        z_s[:, r, :] = sum1[:, r * piece : (r + 1) * piece]
    arrived(r2_r, 13)
    sum2 = jnp.sum(r2_r[...], axis=0) * scale
    for r in range(4):
        z_s[:, 4 + r, :] = sum2[:, r * piece : (r + 1) * piece]
    exchange(z_s, z_r, 10, "dp")
    arrived(q_r, 8)
    for r in range(4):
        gfil[:, r * lanes : (r + 1) * lanes] = q_r[:, r, :]
    gskip[...] = jnp.sum(q_r[:, 4, :].T, axis=0, keepdims=True)
    arrived(z_r, 10)
    a_s[...] = jnp.sum(z_r[...], axis=0)
    exchange(a_s, a_r, 11, gather=True)
    arrived(a_r, 11)

    def line(r):
        return jnp.concatenate([a_r[:, r, :], a_r[:, r + 1, :]], axis=1)

    gout[...] = line(2)
    for k, r in enumerate((0, 4, 6)):
        h, m, t = split3(line(r))
        gin[:, k * width : (k + 1) * width] = dot(h, perm) + (dot(m, perm) + dot(t, perm))

    for slot, ref in (
        (0, tap_r),
        (1, gat_r),
        (2, dcn_r),
        (3, con_r),
        (4, dga_r),
        (5, gf_r),
        (6, sk_r),
        (8, q_r),
        (10, z_r),
        (11, a_r),
        (12, r1_r),
        (13, r2_r),
    ):
        sent(ref, slot)
    for slot, ref in ((7, p1_r), (9, p2_r)):
        pltpu.make_async_copy(ref, ref, send.at[slot]).wait()


def deliver(*refs):
    half = len(refs) // 2
    for src, dst in zip(refs[:half], refs[half:]):
        dst[...] = src[...]


def shards(tokens, cotangent, w_in, w_out, filter_taps, skip):
    seq_n, dp_n = lax.axis_size("seq"), lax.axis_size("dp")
    block, width = tokens.shape[1:]
    chans = width // seq_n
    scale = 1.0 / math.sqrt(dp_n * seq_n * block)
    own = width // dp_n

    def shape(*dims, dtype=F32):
        return pltpu.VMEM(dims, dtype)

    ex = (seq_n, chans, block)
    sp = (seq_n, chans, 2 * block)
    scratch = [
        *[shape(*ex)] * 6,
        shape(3 * width, block),
        shape(width, block),
        shape(3 * width, width, dtype=BF16),
        shape(width, width, dtype=BF16),
        shape(width, block, dtype=BF16),
        shape(3 * block, 2 * block, dtype=BF16),
        shape(6 * block, block, dtype=BF16),
        *[shape(*sp)] * 4,
        *[shape(*ex)] * 4,
        shape(4, width, block // 4),
        *[shape(dp_n, seq_n, block)] * 2,
        *[shape(dp_n, 8, block // 4)] * 2,
        *[shape(seq_n, 8, block // 4)] * 2,
        shape(3 * width, block, dtype=BF16),
        *[shape(2, seq_n // 2, chans, 2 * width)] * 2,
        *[shape(seq_n // 2, chans, 2 * width)] * 6,
        *[shape(dp_n, 8, width // 2)] * 2,
        shape(8, width // 2),
        shape(seq_n, 8, width // 2),
        pltpu.SemaphoreType.DMA((14,)),
        pltpu.SemaphoreType.DMA((14,)),
    ]
    vmem = pl.BlockSpec(memory_space=pltpu.VMEM)
    results = pl.pallas_call(
        functools.partial(body, seq_n, dp_n, scale),
        out_shape=(
            jax.ShapeDtypeStruct((block, width), BF16),
            jax.ShapeDtypeStruct((block, width), BF16),
            jax.ShapeDtypeStruct((own, 3 * width), F32),
            jax.ShapeDtypeStruct((own, width), F32),
            jax.ShapeDtypeStruct((own, block), F32),
            jax.ShapeDtypeStruct((1, own), F32),
        ),
        in_specs=[vmem] * 7,
        out_specs=(vmem,) * 6,
        scratch_shapes=scratch,
        compiler_params=pltpu.CompilerParams(
            collective_id=0, has_side_effects=True, vmem_limit_bytes=56 * 1024 * 1024
        ),
        name="operator",
    )(tokens[0], cotangent[0], w_in, w_out, filter_taps, skip[None], jnp.asarray(tables(block)))
    out, dinp, gin, gout, gfil, gskip = pl.pallas_call(
        deliver,
        out_shape=tuple(jax.ShapeDtypeStruct(r.shape, r.dtype) for r in results),
        in_specs=[vmem] * 6,
        out_specs=(vmem,) * 6,
        name="deliver",
    )(*results)
    return out[None], dinp[None], gin, gout, gfil.T, gskip[0]


def solution(mesh):
    return jax.shard_map(
        shards,
        mesh=mesh,
        in_specs=(P("dp", "seq", None), P("dp", "seq", None), P(), P(), P("seq", None), P()),
        out_specs=(
            P("dp", "seq", None),
            P("dp", "seq", None),
            P("dp", None),
            P("dp", None),
            P("seq", "dp"),
            P("dp"),
        ),
        check_vma=False,
    )
```

```python
import functools
import math

import jax
import jax.numpy as jnp
import numpy as np
from jax import lax
from jax.experimental import pallas as pl
from jax.experimental.pallas import tpu as pltpu
from jax.sharding import PartitionSpec as P

F32 = jnp.float32
BF16 = jnp.bfloat16
ROWS = 16
NT = (((1,), (1,)), ((), ()))
TN = (((0,), (0,)), ((), ()))


def tables(block):
    def turn(numer):
        angle = np.pi / (2 * block) * (numer % (4 * block))
        return np.cos(angle), np.sin(angle)

    pos = np.arange(block)
    coarse = np.arange(block // ROWS) * ROWS
    fine = np.arange(ROWS)
    odd = 2 * pos + 1
    parts = [
        *turn(np.outer(coarse, odd)),
        *turn(np.outer(fine, odd)),
        *turn(np.outer(2 * coarse, pos)),
        *turn(np.outer(2 * fine + 1, pos)),
    ]
    return np.concatenate(parts, axis=0).astype(np.float32)


def split2(x):
    high = x.astype(BF16)
    return high, (x - high.astype(F32)).astype(BF16)


def split3(x):
    high = x.astype(BF16)
    rest = x - high.astype(F32)
    mid = rest.astype(BF16)
    return high, mid, (rest - mid.astype(F32)).astype(BF16)


def dot(a, b, dims=(((1,), (0,)), ((), ()))):
    return lax.dot_general(a, b, dims, preferred_element_type=F32)


def block_conv(p_ref, q_ref, o_ref, block, size, corr, first, groups):
    total = q_ref.shape[0] // size
    lanes = min(128, block)

    def tile(t, _):
        re = pl.ds(pl.multiple_of(t * lanes, lanes), lanes)
        im = pl.ds(pl.multiple_of(block + t * lanes, lanes), lanes)

        def chunk(acc, out0, in0, diag):
            acc = list(acc)
            cache = {}
            base = in0 - out0 if corr else out0 - in0
            for u in range(size):
                qr, qi = q_ref[in0 + u, :, re], q_ref[in0 + u, :, im]
                qs = qr + qi
                for r in range(size):
                    lag = u - r if corr else r - u
                    if diag and lag < 0:
                        continue
                    if lag not in cache:
                        pr, pi = p_ref[base + lag, :, re], p_ref[base + lag, :, im]
                        both, diff = pr + pi, pi - pr
                        cache[lag] = (pr, -both, -diff) if corr else (pr, diff, both)
                    one, two, three = cache[lag]
                    acc[3 * r] = acc[3 * r] + one * qs
                    acc[3 * r + 1] = acc[3 * r + 1] + two * qr
                    acc[3 * r + 2] = acc[3 * r + 2] + three * qi
            return tuple(acc)

        def group(g, _):
            out0 = g * size
            zero = jnp.zeros((q_ref.shape[1], lanes), F32)
            acc = chunk((zero,) * (3 * size), out0, out0, True)

            def step(h, acc):
                return chunk(acc, out0, h * size, False)

            low, top = (g + 1, total) if corr else (0, g)
            acc = lax.fori_loop(low, top, step, acc)
            for r in range(size):
                o_ref[out0 + r, :, re] = acc[3 * r] - acc[3 * r + 2]
                o_ref[out0 + r, :, im] = acc[3 * r] + acc[3 * r + 1]
            return 0

        lax.fori_loop(first, first + groups, group, 0)
        return 0

    lax.fori_loop(0, block // lanes, tile, 0)


def farthest_first(step, mine, parts, ring):
    if ring:
        back = step % 2
        return (mine + back * (parts - (step + 1) // 2) + (1 - back) * (step // 2)) % parts

    def offset(i):
        return (i * (i + 1) // 2) % 4

    cores = parts // 16
    if cores == 0:
        return (mine + step) % parts
    chip = mine // cores
    x, y = chip // 4 + offset(step // (4 * cores)), chip % 4 + offset((step // cores) % 4)
    return ((x % 4) * 4 + y % 4) * cores + (mine + step) % cores


def body(
    seq_n,
    dp_n,
    scale,
    tok,
    cot,
    w_in,
    w_out,
    taps,
    skip,
    tab,
    out,
    dinp,
    gin,
    gout,
    gfil,
    gskip,
    tap_s,
    gat_s,
    dcn_s,
    tap_r,
    gat_r,
    dcn_r,
    proj,
    dmx,
    w_t,
    w_o,
    tok_t,
    f_mat,
    b_mat,
    h_sp,
    x_sp,
    d_sp,
    o_sp,
    con_s,
    dga_s,
    con_r,
    dga_r,
    gf_t,
    gf_s,
    gf_r,
    sk_s,
    sk_r,
    q_s,
    q_r,
    dproj,
    g1_s,
    g2_s,
    p1_r,
    p2_r,
    r1_s,
    r2_s,
    r1_r,
    r2_r,
    z_s,
    z_r,
    a_s,
    a_r,
    send,
    recv,
):
    block, width = tok.shape
    chans = width // seq_n
    me = lax.axis_index("seq")
    my_dp = lax.axis_index("dp")
    core = lax.rem(me, 2)
    group = 8 if seq_n >= 32 else 2

    barrier = pltpu.get_barrier_semaphore()

    def greet_seq(k, _):
        peer = farthest_first(seq_n - k, me, seq_n, False)
        pl.semaphore_signal(barrier, 1, device_id={"seq": peer})
        return 0

    def greet_dp(k, _):
        peer = farthest_first(dp_n - k, my_dp, dp_n, True)
        pl.semaphore_signal(barrier, 1, device_id={"dp": peer})
        return 0

    lax.fori_loop(1, seq_n, greet_seq, 0)
    lax.fori_loop(1, dp_n, greet_dp, 0)

    def exchange(src, dst, slot, axis="seq", gather=False, cores=1):
        mine, parts = (me // cores, seq_n // cores) if axis == "seq" else (my_dp, dp_n)
        own = src if gather else src.at[mine]
        pltpu.make_async_copy(own, dst.at[mine], recv.at[slot]).start()

        def go(k, _):
            peer = farthest_first(parts - k, mine, parts, axis == "dp")
            pltpu.make_async_remote_copy(
                src if gather else src.at[peer],
                dst.at[mine],
                send.at[slot],
                recv.at[slot],
                device_id={axis: peer if cores == 1 else peer * cores + core},
            ).start()
            return 0

        lax.fori_loop(1, parts, go, 0)

    half_n = seq_n // 2

    def half_exchange(src, dst, slot, half, own):
        if own:
            pltpu.make_async_copy(src.at[me], dst.at[me], recv.at[slot]).start()

        def go(k, _):
            step = half_n - 1 - k
            if half_n == 16:
                x, y = (me // 8 + step // 8) % 2, (me // 2 + (step // 2) * (step // 2 + 1) // 2) % 4
                peer = half * half_n + x * 8 + y * 2 + (me + step) % 2
            else:
                peer = half * half_n + (me + step) % half_n
            pltpu.make_async_remote_copy(
                src.at[peer],
                dst.at[me],
                send.at[slot],
                recv.at[slot],
                device_id={"seq": peer},
            ).start()
            return 0

        lax.fori_loop(0, half_n - 1 if own else half_n, go, 0)

    def swap(src, dst, slot):
        pltpu.make_async_remote_copy(
            src.at[1 - core],
            dst,
            send.at[slot],
            recv.at[slot],
            device_id={"seq": me + 1 - 2 * core},
        ).start()

    def arrived(dst, slot):
        pltpu.make_async_copy(dst, dst, recv.at[slot]).wait()

    def sent(dst, slot):
        rest = dst.at[pl.ds(0, dst.shape[0] - 1)]
        pltpu.make_async_copy(rest, rest, send.at[slot]).wait()

    row = lax.broadcasted_iota(jnp.int32, (width, width), 0)
    col = lax.broadcasted_iota(jnp.int32, (width, width), 1)
    hit = (col % seq_n) * chans + col // seq_n == row
    perm = jnp.where(hit, 1.0, 0.0).astype(BF16)
    skip_col = jnp.sum(jnp.where(hit, skip[...], 0.0), axis=1, keepdims=True)

    high, low = split2(taps[...])
    taps_t = dot(perm, high, NT) + dot(perm, low, NT)
    tap_s[...] = taps_t.reshape(seq_n, chans, block)

    for part in range(3):
        rows = pl.ds(part * width, width)
        w_t[rows, :] = dot(perm, w_in[:, part * width : (part + 1) * width], NT).astype(BF16)
        proj[rows, :] = dot(w_t[rows, :], tok[...], NT)
    gate_out = proj.at[pl.ds(0, width)]
    gate_in = proj.at[pl.ds(width, width)]
    values = proj.at[pl.ds(2 * width, width)]
    gat_s[...] = (values[...] * gate_in[...]).reshape(seq_n, chans, block)

    w_o[...] = dot(perm, w_out[...]).astype(BF16)
    dmx[...] = dot(w_o[...], cot[...], NT)
    dcn_s[...] = (dmx[...] * gate_out[...]).reshape(seq_n, chans, block)
    pl.semaphore_wait(barrier, seq_n + dp_n - 2)
    exchange(tap_s, tap_r, 0)
    exchange(gat_s, gat_r, 1)
    exchange(dcn_s, dcn_r, 2)
    tok_t[...] = dot(perm, tok[...], NT).astype(BF16)

    big = block // ROWS

    def build(dst, first, vertical):
        cos_f = tab[pl.ds(first + 2 * big, ROWS), :]
        sin_f = tab[pl.ds(first + 2 * big + ROWS, ROWS), :]

        def rows_of(a, _):
            cos_c = tab[pl.ds(first + a, 1), :]
            sin_c = tab[pl.ds(first + big + a, 1), :]
            cos = cos_c * cos_f - sin_c * sin_f
            sin = -(sin_c * cos_f + cos_c * sin_f)
            at = pl.multiple_of(a * ROWS, ROWS)
            for k, value in enumerate((cos, sin)):
                high, low = split2(value)
                for copy, piece in enumerate((high, low) if vertical else (high, high, low)):
                    if vertical:
                        dst[pl.ds((2 * copy + k) * block + at, ROWS), :] = piece
                    else:
                        dst[pl.ds(copy * block + at, ROWS), k * block : (k + 1) * block] = piece
            return 0

        lax.fori_loop(0, big, rows_of, 0)

    build(f_mat, 0, False)
    build(b_mat, 2 * big + 2 * ROWS, True)

    rows_n = seq_n * chans
    step = min(256, block)

    def spectrum(src, dst):
        high, low = split2(src[...].reshape(rows_n, block))
        wide = jnp.concatenate([high, low, high], axis=1)
        for n in range(0, 2 * block, step):
            dst[:, :, n : n + step] = dot(wide, f_mat[:, n : n + step]).reshape(seq_n, chans, step)

    def field(first, factor):
        rows = half_n * chans
        high, low = split2(o_sp[pl.ds(first, half_n)].reshape(rows, 2 * block))
        wide = dot(jnp.concatenate([high, low], axis=0), b_mat[: 2 * block, :])
        return (wide[:rows] + wide[rows:] + dot(high, b_mat[2 * block :, :])) * factor

    odd = lax.broadcasted_iota(jnp.int32, (1, 1, block), 2) % 2
    sign = (1 - 2 * odd).astype(F32)

    arrived(tap_r, 0)
    spectrum(tap_r, o_sp)
    h_sp[0] = o_sp[0]
    h_sp[1:, :, :block] = o_sp[1:, :, :block] - sign * o_sp[: seq_n - 1, :, block:]
    h_sp[1:, :, block:] = o_sp[1:, :, block:] + sign * o_sp[: seq_n - 1, :, :block]

    arrived(gat_r, 1)
    spectrum(gat_r, x_sp)
    groups = half_n // group
    mine = me // half_n

    def send_back(q_sp, src, dst, slot, corr):
        for own in (False, True):
            half = mine if own else 1 - mine
            first = half * half_n
            block_conv(h_sp, q_sp, o_sp, block, group, corr, half * groups, groups)
            src[pl.ds(first, half_n)] = field(first, 1.0 / block).reshape(half_n, chans, block)
            half_exchange(src, dst, slot, half, own)

    send_back(x_sp, con_s, con_r, 3, False)
    arrived(dcn_r, 2)
    spectrum(dcn_r, d_sp)
    send_back(d_sp, dga_s, dga_r, 4, True)

    lanes = block // 4
    for half in (1, 0):
        first, end = half * half_n, (half + 1) * half_n
        block_conv(x_sp, d_sp, h_sp, block, group, True, half * groups, groups)
        if half:
            end = end - 1
            o_sp[end] = h_sp[end]
        o_sp[first:end, :, :block] = h_sp[first:end, :, :block] + sign * h_sp[first + 1 : end + 1, :, block:]
        o_sp[first:end, :, block:] = h_sp[first:end, :, block:] - sign * h_sp[first + 1 : end + 1, :, :block]
        term = field(first, scale / block)
        for r in range(4):
            gf_t[r] = term[:, r * lanes : (r + 1) * lanes]
            for d in range(dp_n):
                gf_s[half, d, :, r * lanes : (r + 1) * lanes] = gf_t[r, pl.ds(d, half_n, stride=chans), :]
        exchange(gf_s.at[half], gf_r.at[half], 5 + 9 * half, "dp")
    both = jnp.sum(gat_r[...] * dcn_r[...], axis=0)
    narrow = both[:, :lanes]
    for r in range(1, 4):
        narrow = narrow + both[:, r * lanes : (r + 1) * lanes]
    for d in range(dp_n):
        sk_s[d] = jnp.broadcast_to(narrow[d : d + 1, :], (8, lanes))
    exchange(sk_s, sk_r, 6, "dp")

    arrived(con_r, 3)
    gated = gat_s[...].reshape(width, block)
    conv = con_r[...].reshape(width, block) + skip_col * gated
    mixed = (conv * gate_out[...]).astype(BF16)
    dproj[pl.ds(0, width), :] = (dmx[...] * conv).astype(BF16)

    def fill(dst, first, term):
        term = term.reshape(seq_n // 2, 2, chans, width)
        for c in (0, 1):
            dst[c, :, :, first : first + width] = term[:, c]

    fill(g1_s, 0, dot(tok_t[...], dproj[pl.ds(0, width), :], NT))
    fill(g1_s, width, dot(mixed, cot[...]))
    swap(g1_s, p1_r, 7)
    out[...] = dot(mixed, w_o[...], TN).astype(BF16)
    arrived(p1_r, 7)
    r1_s[...] = g1_s[core] + p1_r[...]
    exchange(r1_s, r1_r, 12, cores=2)

    arrived(dga_r, 4)
    dgated = dga_r[...].reshape(width, block) + skip_col * dcn_s[...].reshape(width, block)
    dproj[pl.ds(width, width), :] = (dgated * values[...]).astype(BF16)
    dproj[pl.ds(2 * width, width), :] = (dgated * gate_in[...]).astype(BF16)
    for k in (0, 1):
        fill(g2_s, k * width, dot(tok_t[...], dproj[pl.ds((k + 1) * width, width), :], NT))
    swap(g2_s, p2_r, 9)
    arrived(p2_r, 9)
    r2_s[...] = g2_s[core] + p2_r[...]
    exchange(r2_s, r2_r, 13, cores=2)
    dinp[...] = dot(dproj[...], w_t[...], TN).astype(BF16)

    arrived(sk_r, 6)
    sk_sum = jnp.sum(sk_r[...], axis=0) * scale
    for half in (1, 0):
        arrived(gf_r.at[half], 5 + 9 * half)
        gf_sum = jnp.sum(gf_r[half], axis=0)
        for r in range(4):
            q_s[half * half_n : (half + 1) * half_n, r, :] = gf_sum[:, r * lanes : (r + 1) * lanes]
    q_s[:, 4, :] = jnp.broadcast_to(sk_sum[0:1, :], (seq_n, lanes))
    exchange(q_s, q_r, 8)

    arrived(r1_r, 12)
    sum1 = jnp.sum(r1_r[...], axis=0) * scale
    piece = 2 * width // 4
    for r in range(4):
        z_s[:, r, :] = sum1[:, r * piece : (r + 1) * piece]
    arrived(r2_r, 13)
    sum2 = jnp.sum(r2_r[...], axis=0) * scale
    for r in range(4):
        z_s[:, 4 + r, :] = sum2[:, r * piece : (r + 1) * piece]
    exchange(z_s, z_r, 10, "dp")
    arrived(q_r, 8)
    for r in range(4):
        gfil[:, r * lanes : (r + 1) * lanes] = q_r[:, r, :]
    gskip[...] = jnp.sum(q_r[:, 4, :].T, axis=0, keepdims=True)
    arrived(z_r, 10)
    a_s[...] = jnp.sum(z_r[...], axis=0)
    exchange(a_s, a_r, 11, gather=True)
    arrived(a_r, 11)

    def line(r):
        return jnp.concatenate([a_r[:, r, :], a_r[:, r + 1, :]], axis=1)

    gout[...] = line(2)
    for k, r in enumerate((0, 4, 6)):
        h, m, t = split3(line(r))
        gin[:, k * width : (k + 1) * width] = dot(h, perm) + (dot(m, perm) + dot(t, perm))

    for slot, ref in (
        (0, tap_r),
        (1, gat_r),
        (2, dcn_r),
        (3, con_r),
        (4, dga_r),
        (5, gf_r.at[0]),
        (14, gf_r.at[1]),
        (6, sk_r),
        (8, q_r),
        (10, z_r),
        (11, a_r),
        (12, r1_r),
        (13, r2_r),
    ):
        sent(ref, slot)
    for slot, ref in ((7, p1_r), (9, p2_r)):
        pltpu.make_async_copy(ref, ref, send.at[slot]).wait()


def deliver(*refs):
    half = len(refs) // 2
    for src, dst in zip(refs[:half], refs[half:]):
        dst[...] = src[...]


def shards(tokens, cotangent, w_in, w_out, filter_taps, skip):
    seq_n, dp_n = lax.axis_size("seq"), lax.axis_size("dp")
    block, width = tokens.shape[1:]
    chans = width // seq_n
    scale = 1.0 / math.sqrt(dp_n * seq_n * block)
    own = width // dp_n

    def shape(*dims, dtype=F32):
        return pltpu.VMEM(dims, dtype)

    ex = (seq_n, chans, block)
    sp = (seq_n, chans, 2 * block)
    scratch = [
        *[shape(*ex)] * 6,
        shape(3 * width, block),
        shape(width, block),
        shape(3 * width, width, dtype=BF16),
        shape(width, width, dtype=BF16),
        shape(width, block, dtype=BF16),
        shape(3 * block, 2 * block, dtype=BF16),
        shape(4 * block, block, dtype=BF16),
        *[shape(*sp)] * 4,
        *[shape(*ex)] * 4,
        shape(4, width // 2, block // 4),
        *[shape(2, dp_n, seq_n // 2, block)] * 2,
        *[shape(dp_n, 8, block // 4)] * 2,
        *[shape(seq_n, 8, block // 4)] * 2,
        shape(3 * width, block, dtype=BF16),
        *[shape(2, seq_n // 2, chans, 2 * width)] * 2,
        *[shape(seq_n // 2, chans, 2 * width)] * 6,
        *[shape(dp_n, 8, width // 2)] * 2,
        shape(8, width // 2),
        shape(seq_n, 8, width // 2),
        pltpu.SemaphoreType.DMA((15,)),
        pltpu.SemaphoreType.DMA((15,)),
    ]
    vmem = pl.BlockSpec(memory_space=pltpu.VMEM)
    results = pl.pallas_call(
        functools.partial(body, seq_n, dp_n, scale),
        out_shape=(
            jax.ShapeDtypeStruct((block, width), BF16),
            jax.ShapeDtypeStruct((block, width), BF16),
            jax.ShapeDtypeStruct((own, 3 * width), F32),
            jax.ShapeDtypeStruct((own, width), F32),
            jax.ShapeDtypeStruct((own, block), F32),
            jax.ShapeDtypeStruct((1, own), F32),
        ),
        in_specs=[vmem] * 7,
        out_specs=(vmem,) * 6,
        scratch_shapes=scratch,
        compiler_params=pltpu.CompilerParams(
            collective_id=0, has_side_effects=True, vmem_limit_bytes=56 * 1024 * 1024
        ),
        name="operator",
    )(tokens[0], cotangent[0], w_in, w_out, filter_taps, skip[None], jnp.asarray(tables(block)))
    out, dinp, gin, gout, gfil, gskip = pl.pallas_call(
        deliver,
        out_shape=tuple(jax.ShapeDtypeStruct(r.shape, r.dtype) for r in results),
        in_specs=[vmem] * 6,
        out_specs=(vmem,) * 6,
        name="deliver",
    )(*results)
    return out[None], dinp[None], gin, gout, gfil.T, gskip[0]


def solution(mesh):
    return jax.shard_map(
        shards,
        mesh=mesh,
        in_specs=(P("dp", "seq", None), P("dp", "seq", None), P(), P(), P("seq", None), P()),
        out_specs=(
            P("dp", "seq", None),
            P("dp", "seq", None),
            P("dp", None),
            P("dp", None),
            P("seq", "dp"),
            P("dp"),
        ),
        check_vma=False,
    )
```

```python
import functools
import math

import jax
import jax.numpy as jnp
import numpy as np
from jax import lax
from jax.experimental import pallas as pl
from jax.experimental.pallas import tpu as pltpu
from jax.sharding import PartitionSpec as P

F32 = jnp.float32
BF16 = jnp.bfloat16
ROWS = 16
NT = (((1,), (1,)), ((), ()))
TN = (((0,), (0,)), ((), ()))


def tables(block):
    def turn(numer):
        angle = np.pi / (2 * block) * (numer % (4 * block))
        return np.cos(angle), np.sin(angle)

    pos = np.arange(block)
    coarse = np.arange(block // ROWS) * ROWS
    fine = np.arange(ROWS)
    odd = 2 * pos + 1
    parts = [
        *turn(np.outer(coarse, odd)),
        *turn(np.outer(fine, odd)),
        *turn(np.outer(2 * coarse, pos)),
        *turn(np.outer(2 * fine + 1, pos)),
    ]
    return np.concatenate(parts, axis=0).astype(np.float32)


def split2(x):
    high = x.astype(BF16)
    return high, (x - high.astype(F32)).astype(BF16)


def split3(x):
    high = x.astype(BF16)
    rest = x - high.astype(F32)
    mid = rest.astype(BF16)
    return high, mid, (rest - mid.astype(F32)).astype(BF16)


def dot(a, b, dims=(((1,), (0,)), ((), ()))):
    return lax.dot_general(a, b, dims, preferred_element_type=F32)


def block_conv(p_ref, q_ref, o_ref, block, size, corr, first, groups):
    total = q_ref.shape[0] // size
    lanes = min(128, block)

    def tile(t, _):
        re = pl.ds(pl.multiple_of(t * lanes, lanes), lanes)
        im = pl.ds(pl.multiple_of(block + t * lanes, lanes), lanes)

        def chunk(acc, out0, in0, diag):
            acc = list(acc)
            cache = {}
            base = in0 - out0 if corr else out0 - in0
            for u in range(size):
                qr, qi = q_ref[in0 + u, :, re], q_ref[in0 + u, :, im]
                qs = qr + qi
                for r in range(size):
                    lag = u - r if corr else r - u
                    if diag and lag < 0:
                        continue
                    if lag not in cache:
                        pr, pi = p_ref[base + lag, :, re], p_ref[base + lag, :, im]
                        both, diff = pr + pi, pi - pr
                        cache[lag] = (pr, -both, -diff) if corr else (pr, diff, both)
                    one, two, three = cache[lag]
                    acc[3 * r] = acc[3 * r] + one * qs
                    acc[3 * r + 1] = acc[3 * r + 1] + two * qr
                    acc[3 * r + 2] = acc[3 * r + 2] + three * qi
            return tuple(acc)

        def group(g, _):
            out0 = g * size
            zero = jnp.zeros((q_ref.shape[1], lanes), F32)
            acc = chunk((zero,) * (3 * size), out0, out0, True)

            def step(h, acc):
                return chunk(acc, out0, h * size, False)

            low, top = (g + 1, total) if corr else (0, g)
            acc = lax.fori_loop(low, top, step, acc)
            for r in range(size):
                o_ref[out0 + r, :, re] = acc[3 * r] - acc[3 * r + 2]
                o_ref[out0 + r, :, im] = acc[3 * r] + acc[3 * r + 1]
            return 0

        lax.fori_loop(first, first + groups, group, 0)
        return 0

    lax.fori_loop(0, block // lanes, tile, 0)


def farthest_first(step, mine, parts, ring):
    if ring:
        back = step % 2
        return (mine + back * (parts - (step + 1) // 2) + (1 - back) * (step // 2)) % parts

    def offset(i):
        return (i * (i + 1) // 2) % 4

    cores = parts // 16
    if cores == 0:
        return (mine + step) % parts
    chip = mine // cores
    x, y = chip // 4 + offset(step // (4 * cores)), chip % 4 + offset((step // cores) % 4)
    return ((x % 4) * 4 + y % 4) * cores + (mine + step) % cores


def body(
    seq_n,
    dp_n,
    scale,
    tok,
    cot,
    w_in,
    w_out,
    taps,
    skip,
    tab,
    out,
    dinp,
    gin,
    gout,
    gfil,
    gskip,
    tap_s,
    gat_s,
    dcn_s,
    tap_r,
    gat_r,
    dcn_r,
    proj,
    dmx,
    w_t,
    w_o,
    tok_t,
    f_mat,
    b_mat,
    h_sp,
    x_sp,
    d_sp,
    o_sp,
    con_s,
    dga_s,
    con_r,
    dga_r,
    gf_t,
    gf_s,
    gf_r,
    sk_s,
    sk_r,
    q_s,
    q_r,
    dproj,
    g1_s,
    g2_s,
    p1_r,
    p2_r,
    r1_s,
    r2_s,
    r1_r,
    r2_r,
    z_s,
    z_r,
    a_s,
    a_r,
    send,
    recv,
):
    block, width = tok.shape
    chans = width // seq_n
    me = lax.axis_index("seq")
    my_dp = lax.axis_index("dp")
    core = lax.rem(me, 2)
    group = 8 if seq_n >= 32 else 2

    barrier = pltpu.get_barrier_semaphore()

    def greet_seq(k, _):
        peer = farthest_first(seq_n - k, me, seq_n, False)
        pl.semaphore_signal(barrier, 1, device_id={"seq": peer})
        return 0

    def greet_dp(k, _):
        peer = farthest_first(dp_n - k, my_dp, dp_n, True)
        pl.semaphore_signal(barrier, 1, device_id={"dp": peer})
        return 0

    lax.fori_loop(1, seq_n, greet_seq, 0)
    lax.fori_loop(1, dp_n, greet_dp, 0)

    def exchange(src, dst, slot, axis="seq", gather=False, cores=1):
        mine, parts = (me // cores, seq_n // cores) if axis == "seq" else (my_dp, dp_n)
        own = src if gather else src.at[mine]
        pltpu.make_async_copy(own, dst.at[mine], recv.at[slot]).start()

        def go(k, _):
            peer = farthest_first(parts - k, mine, parts, axis == "dp")
            pltpu.make_async_remote_copy(
                src if gather else src.at[peer],
                dst.at[mine],
                send.at[slot],
                recv.at[slot],
                device_id={axis: peer if cores == 1 else peer * cores + core},
            ).start()
            return 0

        lax.fori_loop(1, parts, go, 0)

    half_n = seq_n // 2

    def half_exchange(src, dst, slot, half, own):
        if own:
            pltpu.make_async_copy(src.at[me], dst.at[me], recv.at[slot]).start()

        def go(k, _):
            step = half_n - 1 - k
            if half_n == 16:
                x, y = (me // 8 + step // 8) % 2, (me // 2 + (step // 2) * (step // 2 + 1) // 2) % 4
                peer = half * half_n + x * 8 + y * 2 + (me + step) % 2
            else:
                peer = half * half_n + (me + step) % half_n
            pltpu.make_async_remote_copy(
                src.at[peer],
                dst.at[me],
                send.at[slot],
                recv.at[slot],
                device_id={"seq": peer},
            ).start()
            return 0

        lax.fori_loop(0, half_n - 1 if own else half_n, go, 0)

    def swap(src, dst, slot):
        pltpu.make_async_remote_copy(
            src.at[1 - core],
            dst,
            send.at[slot],
            recv.at[slot],
            device_id={"seq": me + 1 - 2 * core},
        ).start()

    def arrived(dst, slot):
        pltpu.make_async_copy(dst, dst, recv.at[slot]).wait()

    def sent(dst, slot):
        rest = dst.at[pl.ds(0, dst.shape[0] - 1)]
        pltpu.make_async_copy(rest, rest, send.at[slot]).wait()

    row = lax.broadcasted_iota(jnp.int32, (width, width), 0)
    col = lax.broadcasted_iota(jnp.int32, (width, width), 1)
    hit = (col % seq_n) * chans + col // seq_n == row
    perm = jnp.where(hit, 1.0, 0.0).astype(BF16)

    for part in range(3):
        rows = pl.ds(part * width, width)
        w_t[rows, :] = dot(perm, w_in[:, part * width : (part + 1) * width], NT).astype(BF16)
    high, low = split2(taps[...])
    taps_t = dot(perm, high, NT) + dot(perm, low, NT)
    for h in (0, 1):
        piece = taps_t[:, h * (block // 2) : (h + 1) * (block // 2)]
        tap_s[h] = piece.reshape(seq_n, chans, block // 2)
    gate_out = proj.at[pl.ds(0, width)]
    gate_in = proj.at[pl.ds(width, width)]
    values = proj.at[pl.ds(2 * width, width)]
    gate_in[...] = dot(w_t[pl.ds(width, width), :], tok[...], NT)
    values[...] = dot(w_t[pl.ds(2 * width, width), :], tok[...], NT)
    gat_s[...] = (values[...] * gate_in[...]).reshape(seq_n, chans, block)
    pl.semaphore_wait(barrier, seq_n + dp_n - 2)

    parity = my_dp % 2
    near, far = tap_r.at[parity], tap_r.at[1 - parity]
    exchange(tap_s.at[parity], near, 0)
    exchange(gat_s, gat_r, 1)
    gate_out[...] = dot(w_t[pl.ds(0, width), :], tok[...], NT)
    w_o[...] = dot(perm, w_out[...]).astype(BF16)
    dmx[...] = dot(w_o[...], cot[...], NT)
    dcn_s[...] = (dmx[...] * gate_out[...]).reshape(seq_n, chans, block)
    exchange(dcn_s, dcn_r, 2)
    tok_t[...] = dot(perm, tok[...], NT).astype(BF16)
    skip_col = jnp.sum(jnp.where(hit, skip[...], 0.0), axis=1, keepdims=True)

    big = block // ROWS

    def build(dst, first, vertical):
        cos_f = tab[pl.ds(first + 2 * big, ROWS), :]
        sin_f = tab[pl.ds(first + 2 * big + ROWS, ROWS), :]

        def rows_of(a, _):
            cos_c = tab[pl.ds(first + a, 1), :]
            sin_c = tab[pl.ds(first + big + a, 1), :]
            cos = cos_c * cos_f - sin_c * sin_f
            sin = -(sin_c * cos_f + cos_c * sin_f)
            at = pl.multiple_of(a * ROWS, ROWS)
            for k, value in enumerate((cos, sin)):
                high, low = split2(value)
                for copy, piece in enumerate((high, low) if vertical else (high, high, low)):
                    if vertical:
                        dst[pl.ds((2 * copy + k) * block + at, ROWS), :] = piece
                    else:
                        dst[pl.ds(copy * block + at, ROWS), k * block : (k + 1) * block] = piece
            return 0

        lax.fori_loop(0, big, rows_of, 0)

    build(f_mat, 0, False)
    arrived(near, 0)
    for low, side in ((0, 1), (half_n, dp_n - 1)):
        piece = near.at[pl.ds(low, half_n)]
        pltpu.make_async_remote_copy(
            piece, piece, send.at[15], recv.at[15], device_id={"dp": (my_dp + side) % dp_n}
        ).start()
    build(b_mat, 2 * big + 2 * ROWS, True)

    rows_n = seq_n * chans
    step = min(256, block)

    def spectrum(src, dst):
        high, low = split2(src.reshape(rows_n, block))
        wide = jnp.concatenate([high, low, high], axis=1)
        for n in range(0, 2 * block, step):
            dst[:, :, n : n + step] = dot(wide, f_mat[:, n : n + step]).reshape(seq_n, chans, step)

    def field(first, factor):
        rows = half_n * chans
        high, low = split2(o_sp[pl.ds(first, half_n)].reshape(rows, 2 * block))
        wide = dot(jnp.concatenate([high, low], axis=0), b_mat[: 2 * block, :])
        return (wide[:rows] + wide[rows:] + dot(high, b_mat[2 * block :, :])) * factor

    odd = lax.broadcasted_iota(jnp.int32, (1, 1, block), 2) % 2
    sign = (1 - 2 * odd).astype(F32)

    arrived(gat_r, 1)
    spectrum(gat_r[...], x_sp)
    arrived(far, 15)
    spectrum(jnp.concatenate([tap_r[0], tap_r[1]], axis=2), o_sp)
    h_sp[0] = o_sp[0]
    h_sp[1:, :, :block] = o_sp[1:, :, :block] - sign * o_sp[: seq_n - 1, :, block:]
    h_sp[1:, :, block:] = o_sp[1:, :, block:] + sign * o_sp[: seq_n - 1, :, :block]

    groups = half_n // group
    mine = me // half_n

    def send_back(q_sp, src, dst, slot, corr):
        for own in (False, True):
            half = mine if own else 1 - mine
            first = half * half_n
            block_conv(h_sp, q_sp, o_sp, block, group, corr, half * groups, groups)
            src[pl.ds(first, half_n)] = field(first, 1.0 / block).reshape(half_n, chans, block)
            half_exchange(src, dst, slot, half, own)

    send_back(x_sp, con_s, con_r, 3, False)
    arrived(dcn_r, 2)
    spectrum(dcn_r[...], d_sp)
    send_back(d_sp, dga_s, dga_r, 4, True)

    lanes = block // 4
    for half in (1, 0):
        first, end = half * half_n, (half + 1) * half_n
        block_conv(x_sp, d_sp, h_sp, block, group, True, half * groups, groups)
        if half:
            end = end - 1
            o_sp[end] = h_sp[end]
        o_sp[first:end, :, :block] = h_sp[first:end, :, :block] + sign * h_sp[first + 1 : end + 1, :, block:]
        o_sp[first:end, :, block:] = h_sp[first:end, :, block:] - sign * h_sp[first + 1 : end + 1, :, :block]
        term = field(first, scale / block)
        for r in range(4):
            gf_t[r] = term[:, r * lanes : (r + 1) * lanes]
            for d in range(dp_n):
                gf_s[half, d, :, r * lanes : (r + 1) * lanes] = gf_t[r, pl.ds(d, half_n, stride=chans), :]
        exchange(gf_s.at[half], gf_r.at[half], 5 + 9 * half, "dp")
    both = jnp.sum(gat_r[...] * dcn_r[...], axis=0)
    narrow = both[:, :lanes]
    for r in range(1, 4):
        narrow = narrow + both[:, r * lanes : (r + 1) * lanes]
    for d in range(dp_n):
        sk_s[d] = jnp.broadcast_to(narrow[d : d + 1, :], (8, lanes))
    exchange(sk_s, sk_r, 6, "dp")

    arrived(con_r, 3)
    gated = gat_s[...].reshape(width, block)
    conv = con_r[...].reshape(width, block) + skip_col * gated
    mixed = (conv * gate_out[...]).astype(BF16)
    dproj[pl.ds(0, width), :] = (dmx[...] * conv).astype(BF16)

    def fill(dst, first, term):
        term = term.reshape(seq_n // 2, 2, chans, width)
        for c in (0, 1):
            dst[c, :, :, first : first + width] = term[:, c]

    fill(g1_s, 0, dot(tok_t[...], dproj[pl.ds(0, width), :], NT))
    fill(g1_s, width, dot(mixed, cot[...]))
    swap(g1_s, p1_r, 7)
    out[...] = dot(mixed, w_o[...], TN).astype(BF16)
    arrived(p1_r, 7)
    r1_s[...] = g1_s[core] + p1_r[...]
    exchange(r1_s, r1_r, 12, cores=2)

    arrived(dga_r, 4)
    dgated = dga_r[...].reshape(width, block) + skip_col * dcn_s[...].reshape(width, block)
    dproj[pl.ds(width, width), :] = (dgated * values[...]).astype(BF16)
    dproj[pl.ds(2 * width, width), :] = (dgated * gate_in[...]).astype(BF16)
    for k in (0, 1):
        fill(g2_s, k * width, dot(tok_t[...], dproj[pl.ds((k + 1) * width, width), :], NT))
    swap(g2_s, p2_r, 9)
    arrived(p2_r, 9)
    r2_s[...] = g2_s[core] + p2_r[...]
    exchange(r2_s, r2_r, 13, cores=2)
    dinp[...] = dot(dproj[...], w_t[...], TN).astype(BF16)

    arrived(sk_r, 6)
    sk_sum = jnp.sum(sk_r[...], axis=0) * scale
    for half in (1, 0):
        arrived(gf_r.at[half], 5 + 9 * half)
        gf_sum = jnp.sum(gf_r[half], axis=0)
        for r in range(4):
            q_s[half * half_n : (half + 1) * half_n, r, :] = gf_sum[:, r * lanes : (r + 1) * lanes]
    q_s[:, 4, :] = jnp.broadcast_to(sk_sum[0:1, :], (seq_n, lanes))
    exchange(q_s, q_r, 8)

    arrived(r1_r, 12)
    sum1 = jnp.sum(r1_r[...], axis=0) * scale
    piece = 2 * width // 4
    for r in range(4):
        z_s[:, r, :] = sum1[:, r * piece : (r + 1) * piece]
    arrived(r2_r, 13)
    sum2 = jnp.sum(r2_r[...], axis=0) * scale
    for r in range(4):
        z_s[:, 4 + r, :] = sum2[:, r * piece : (r + 1) * piece]
    exchange(z_s, z_r, 10, "dp")
    arrived(q_r, 8)
    for r in range(4):
        gfil[:, r * lanes : (r + 1) * lanes] = q_r[:, r, :]
    gskip[...] = jnp.sum(q_r[:, 4, :].T, axis=0, keepdims=True)
    arrived(z_r, 10)
    a_s[...] = jnp.sum(z_r[...], axis=0)
    exchange(a_s, a_r, 11, gather=True)
    arrived(a_r, 11)

    def line(r):
        return jnp.concatenate([a_r[:, r, :], a_r[:, r + 1, :]], axis=1)

    gout[...] = line(2)
    for k, r in enumerate((0, 4, 6)):
        h, m, t = split3(line(r))
        gin[:, k * width : (k + 1) * width] = dot(h, perm) + (dot(m, perm) + dot(t, perm))

    for slot, ref in (
        (0, near),
        (1, gat_r),
        (2, dcn_r),
        (3, con_r),
        (4, dga_r),
        (5, gf_r.at[0]),
        (14, gf_r.at[1]),
        (6, sk_r),
        (8, q_r),
        (10, z_r),
        (11, a_r),
        (12, r1_r),
        (13, r2_r),
    ):
        sent(ref, slot)
    for slot, ref in ((7, p1_r), (9, p2_r), (15, near)):
        pltpu.make_async_copy(ref, ref, send.at[slot]).wait()


def deliver(*refs):
    half = len(refs) // 2
    for src, dst in zip(refs[:half], refs[half:]):
        dst[...] = src[...]


def shards(tokens, cotangent, w_in, w_out, filter_taps, skip):
    seq_n, dp_n = lax.axis_size("seq"), lax.axis_size("dp")
    block, width = tokens.shape[1:]
    chans = width // seq_n
    scale = 1.0 / math.sqrt(dp_n * seq_n * block)
    own = width // dp_n

    def shape(*dims, dtype=F32):
        return pltpu.VMEM(dims, dtype)

    ex = (seq_n, chans, block)
    sp = (seq_n, chans, 2 * block)
    scratch = [
        shape(2, seq_n, chans, block // 2),
        *[shape(*ex)] * 2,
        shape(2, seq_n, chans, block // 2),
        *[shape(*ex)] * 2,
        shape(3 * width, block),
        shape(width, block),
        shape(3 * width, width, dtype=BF16),
        shape(width, width, dtype=BF16),
        shape(width, block, dtype=BF16),
        shape(3 * block, 2 * block, dtype=BF16),
        shape(4 * block, block, dtype=BF16),
        *[shape(*sp)] * 4,
        *[shape(*ex)] * 4,
        shape(4, width // 2, block // 4),
        *[shape(2, dp_n, seq_n // 2, block)] * 2,
        *[shape(dp_n, 8, block // 4)] * 2,
        *[shape(seq_n, 8, block // 4)] * 2,
        shape(3 * width, block, dtype=BF16),
        *[shape(2, seq_n // 2, chans, 2 * width)] * 2,
        *[shape(seq_n // 2, chans, 2 * width)] * 6,
        *[shape(dp_n, 8, width // 2)] * 2,
        shape(8, width // 2),
        shape(seq_n, 8, width // 2),
        pltpu.SemaphoreType.DMA((16,)),
        pltpu.SemaphoreType.DMA((16,)),
    ]
    vmem = pl.BlockSpec(memory_space=pltpu.VMEM)
    anywhere = pl.BlockSpec(memory_space=pl.ANY)
    results = pl.pallas_call(
        functools.partial(body, seq_n, dp_n, scale),
        out_shape=(
            jax.ShapeDtypeStruct((block, width), BF16),
            jax.ShapeDtypeStruct((block, width), BF16),
            jax.ShapeDtypeStruct((own, 3 * width), F32),
            jax.ShapeDtypeStruct((own, width), F32),
            jax.ShapeDtypeStruct((own, block), F32),
            jax.ShapeDtypeStruct((1, own), F32),
        ),
        in_specs=[vmem] * 7,
        out_specs=(vmem,) * 6,
        scratch_shapes=scratch,
        compiler_params=pltpu.CompilerParams(
            collective_id=0, has_side_effects=True, vmem_limit_bytes=56 * 1024 * 1024
        ),
        name="operator",
    )(tokens[0], cotangent[0], w_in, w_out, filter_taps, skip[None], jnp.asarray(tables(block)))
    out, dinp, gin, gout, gfil, gskip = pl.pallas_call(
        deliver,
        out_shape=tuple(jax.ShapeDtypeStruct(r.shape, r.dtype) for r in results),
        in_specs=[vmem] * 6,
        out_specs=(vmem,) * 6,
        name="deliver",
    )(*results)
    return out[None], dinp[None], gin, gout, gfil.T, gskip[0]


def solution(mesh):
    return jax.shard_map(
        shards,
        mesh=mesh,
        in_specs=(P("dp", "seq", None), P("dp", "seq", None), P(), P(), P("seq", None), P()),
        out_specs=(
            P("dp", "seq", None),
            P("dp", "seq", None),
            P("dp", None),
            P("dp", None),
            P("seq", "dp"),
            P("dp"),
        ),
        check_vma=False,
    )
```

```python
import functools
import math

import jax
import jax.numpy as jnp
import numpy as np
from jax import lax
from jax.experimental import pallas as pl
from jax.experimental.pallas import tpu as pltpu
from jax.sharding import PartitionSpec as P

F32 = jnp.float32
BF16 = jnp.bfloat16
ROWS = 16
NT = (((1,), (1,)), ((), ()))
TN = (((0,), (0,)), ((), ()))


def tables(block):
    def turn(numer):
        angle = np.pi / (2 * block) * (numer % (4 * block))
        return np.cos(angle), np.sin(angle)

    pos = np.arange(block)
    coarse = np.arange(block // ROWS) * ROWS
    fine = np.arange(ROWS)
    odd = 2 * pos + 1
    parts = [
        *turn(np.outer(coarse, odd)),
        *turn(np.outer(fine, odd)),
        *turn(np.outer(2 * coarse, pos)),
        *turn(np.outer(2 * fine + 1, pos)),
    ]
    return np.concatenate(parts, axis=0).astype(np.float32)


def split2(x):
    high = x.astype(BF16)
    return high, (x - high.astype(F32)).astype(BF16)


def split3(x):
    high = x.astype(BF16)
    rest = x - high.astype(F32)
    mid = rest.astype(BF16)
    return high, mid, (rest - mid.astype(F32)).astype(BF16)


def dot(a, b, dims=(((1,), (0,)), ((), ()))):
    return lax.dot_general(a, b, dims, preferred_element_type=F32)


def block_conv(p_ref, q_ref, o_ref, block, size, corr, first, groups):
    total = q_ref.shape[0] // size
    lanes = min(128, block)

    def tile(t, _):
        re = pl.ds(pl.multiple_of(t * lanes, lanes), lanes)
        im = pl.ds(pl.multiple_of(block + t * lanes, lanes), lanes)

        def chunk(acc, out0, in0, diag):
            acc = list(acc)
            cache = {}
            base = in0 - out0 if corr else out0 - in0
            for u in range(size):
                qr, qi = q_ref[in0 + u, :, re], q_ref[in0 + u, :, im]
                qs = qr + qi
                for r in range(size):
                    lag = u - r if corr else r - u
                    if diag and lag < 0:
                        continue
                    if lag not in cache:
                        pr, pi = p_ref[base + lag, :, re], p_ref[base + lag, :, im]
                        both, diff = pr + pi, pi - pr
                        cache[lag] = (pr, -both, -diff) if corr else (pr, diff, both)
                    one, two, three = cache[lag]
                    acc[3 * r] = acc[3 * r] + one * qs
                    acc[3 * r + 1] = acc[3 * r + 1] + two * qr
                    acc[3 * r + 2] = acc[3 * r + 2] + three * qi
            return tuple(acc)

        def group(g, _):
            out0 = g * size
            zero = jnp.zeros((q_ref.shape[1], lanes), F32)
            acc = chunk((zero,) * (3 * size), out0, out0, True)

            def step(h, acc):
                return chunk(acc, out0, h * size, False)

            low, top = (g + 1, total) if corr else (0, g)
            acc = lax.fori_loop(low, top, step, acc)
            for r in range(size):
                o_ref[out0 + r, :, re] = acc[3 * r] - acc[3 * r + 2]
                o_ref[out0 + r, :, im] = acc[3 * r] + acc[3 * r + 1]
            return 0

        lax.fori_loop(first, first + groups, group, 0)
        return 0

    lax.fori_loop(0, block // lanes, tile, 0)


def farthest_first(step, mine, parts, ring):
    if ring:
        back = step % 2
        return (mine + back * (parts - (step + 1) // 2) + (1 - back) * (step // 2)) % parts

    def offset(i):
        return (i * (i + 1) // 2) % 4

    cores = parts // 16
    if cores == 0:
        return (mine + step) % parts
    chip = mine // cores
    x, y = chip // 4 + offset(step // (4 * cores)), chip % 4 + offset((step // cores) % 4)
    return ((x % 4) * 4 + y % 4) * cores + (mine + step) % cores


def body(
    seq_n,
    dp_n,
    scale,
    tok,
    cot,
    w_in,
    w_out,
    taps,
    skip,
    tab,
    out,
    dinp,
    gin,
    gout,
    gfil,
    gskip,
    tap_s,
    gat_s,
    dcn_s,
    tap_r,
    gat_r,
    dcn_r,
    proj,
    dmx,
    w_t,
    w_o,
    tok_t,
    f_mat,
    b_mat,
    h_sp,
    x_sp,
    d_sp,
    o_sp,
    con_s,
    dga_s,
    con_r,
    dga_r,
    gf_t,
    gf_s,
    gf_r,
    sk_s,
    sk_r,
    q_s,
    q_r,
    dproj,
    g1_s,
    g2_s,
    p1_r,
    p2_r,
    r1_s,
    r2_s,
    r1_r,
    r2_r,
    z_s,
    z_r,
    a_s,
    a_r,
    send,
    recv,
):
    block, width = tok.shape
    chans = width // seq_n
    me = lax.axis_index("seq")
    my_dp = lax.axis_index("dp")
    core = lax.rem(me, 2)
    group = 8 if seq_n >= 32 else 2

    barrier = pltpu.get_barrier_semaphore()

    def greet_seq(k, _):
        peer = farthest_first(seq_n - k, me, seq_n, False)
        pl.semaphore_signal(barrier, 1, device_id={"seq": peer})
        return 0

    def greet_dp(k, _):
        peer = farthest_first(dp_n - k, my_dp, dp_n, True)
        pl.semaphore_signal(barrier, 1, device_id={"dp": peer})
        return 0

    lax.fori_loop(1, seq_n, greet_seq, 0)
    lax.fori_loop(1, dp_n, greet_dp, 0)

    def exchange(src, dst, slot, axis="seq", gather=False, cores=1):
        mine, parts = (me // cores, seq_n // cores) if axis == "seq" else (my_dp, dp_n)
        own = src if gather else src.at[mine]
        pltpu.make_async_copy(own, dst.at[mine], recv.at[slot]).start()

        def go(k, _):
            peer = farthest_first(parts - k, mine, parts, axis == "dp")
            pltpu.make_async_remote_copy(
                src if gather else src.at[peer],
                dst.at[mine],
                send.at[slot],
                recv.at[slot],
                device_id={axis: peer if cores == 1 else peer * cores + core},
            ).start()
            return 0

        lax.fori_loop(1, parts, go, 0)

    half_n = seq_n // 2

    def half_exchange(src, dst, slot, half, own):
        if own:
            pltpu.make_async_copy(src.at[me], dst.at[me], recv.at[slot]).start()

        def go(k, _):
            step = half_n - 1 - k
            if half_n == 16:
                x, y = (me // 8 + step // 8) % 2, (me // 2 + (step // 2) * (step // 2 + 1) // 2) % 4
                peer = half * half_n + x * 8 + y * 2 + (me + step) % 2
            else:
                peer = half * half_n + (me + step) % half_n
            pltpu.make_async_remote_copy(
                src.at[peer],
                dst.at[me],
                send.at[slot],
                recv.at[slot],
                device_id={"seq": peer},
            ).start()
            return 0

        lax.fori_loop(0, half_n - 1 if own else half_n, go, 0)

    def swap(src, dst, slot):
        pltpu.make_async_remote_copy(
            src.at[1 - core],
            dst,
            send.at[slot],
            recv.at[slot],
            device_id={"seq": me + 1 - 2 * core},
        ).start()

    def arrived(dst, slot):
        pltpu.make_async_copy(dst, dst, recv.at[slot]).wait()

    def sent(dst, slot):
        rest = dst.at[pl.ds(0, dst.shape[0] - 1)]
        pltpu.make_async_copy(rest, rest, send.at[slot]).wait()

    row = lax.broadcasted_iota(jnp.int32, (width, width), 0)
    col = lax.broadcasted_iota(jnp.int32, (width, width), 1)
    hit = (col % seq_n) * chans + col // seq_n == row
    perm = jnp.where(hit, 1.0, 0.0).astype(BF16)

    high, low = split2(taps[...])
    taps_t = dot(perm, high, NT) + dot(perm, low, NT)
    for h in (0, 1):
        piece = taps_t[:, h * (block // 2) : (h + 1) * (block // 2)]
        tap_s[h] = piece.reshape(seq_n, chans, block // 2)
    pl.semaphore_wait(barrier, seq_n + dp_n - 2)

    parity = my_dp % 2
    near, far = tap_r.at[parity], tap_r.at[1 - parity]
    exchange(tap_s.at[parity], near, 0)
    for part in range(3):
        rows = pl.ds(part * width, width)
        w_t[rows, :] = dot(perm, w_in[:, part * width : (part + 1) * width], NT).astype(BF16)
    gate_out = proj.at[pl.ds(0, width)]
    gate_in = proj.at[pl.ds(width, width)]
    values = proj.at[pl.ds(2 * width, width)]
    gate_in[...] = dot(w_t[pl.ds(width, width), :], tok[...], NT)
    values[...] = dot(w_t[pl.ds(2 * width, width), :], tok[...], NT)
    gat_s[...] = (values[...] * gate_in[...]).reshape(seq_n, chans, block)
    exchange(gat_s, gat_r, 1)
    gate_out[...] = dot(w_t[pl.ds(0, width), :], tok[...], NT)
    w_o[...] = dot(perm, w_out[...]).astype(BF16)
    dmx[...] = dot(w_o[...], cot[...], NT)
    dcn_s[...] = (dmx[...] * gate_out[...]).reshape(seq_n, chans, block)
    exchange(dcn_s, dcn_r, 2)
    tok_t[...] = dot(perm, tok[...], NT).astype(BF16)
    skip_col = jnp.sum(jnp.where(hit, skip[...], 0.0), axis=1, keepdims=True)

    big = block // ROWS

    def build(dst, first, vertical):
        cos_f = tab[pl.ds(first + 2 * big, ROWS), :]
        sin_f = tab[pl.ds(first + 2 * big + ROWS, ROWS), :]

        def rows_of(a, _):
            cos_c = tab[pl.ds(first + a, 1), :]
            sin_c = tab[pl.ds(first + big + a, 1), :]
            cos = cos_c * cos_f - sin_c * sin_f
            sin = -(sin_c * cos_f + cos_c * sin_f)
            at = pl.multiple_of(a * ROWS, ROWS)
            for k, value in enumerate((cos, sin)):
                high, low = split2(value)
                for copy, piece in enumerate((high, low) if vertical else (high, high, low)):
                    if vertical:
                        dst[pl.ds((2 * copy + k) * block + at, ROWS), :] = piece
                    else:
                        dst[pl.ds(copy * block + at, ROWS), k * block : (k + 1) * block] = piece
            return 0

        lax.fori_loop(0, big, rows_of, 0)

    build(f_mat, 0, False)
    arrived(near, 0)
    for low, side in ((0, 1), (half_n, dp_n - 1)):
        piece = near.at[pl.ds(low, half_n)]
        pltpu.make_async_remote_copy(
            piece, piece, send.at[15], recv.at[15], device_id={"dp": (my_dp + side) % dp_n}
        ).start()
    build(b_mat, 2 * big + 2 * ROWS, True)

    rows_n = seq_n * chans
    step = min(256, block)

    def spectrum(src, dst):
        high, low = split2(src.reshape(rows_n, block))
        wide = jnp.concatenate([high, low, high], axis=1)
        for n in range(0, 2 * block, step):
            dst[:, :, n : n + step] = dot(wide, f_mat[:, n : n + step]).reshape(seq_n, chans, step)

    def field(first, factor):
        rows = half_n * chans
        high, low = split2(o_sp[pl.ds(first, half_n)].reshape(rows, 2 * block))
        wide = dot(jnp.concatenate([high, low], axis=0), b_mat[: 2 * block, :])
        return (wide[:rows] + wide[rows:] + dot(high, b_mat[2 * block :, :])) * factor

    odd = lax.broadcasted_iota(jnp.int32, (1, 1, block), 2) % 2
    sign = (1 - 2 * odd).astype(F32)

    arrived(gat_r, 1)
    spectrum(gat_r[...], x_sp)
    arrived(far, 15)
    spectrum(jnp.concatenate([tap_r[0], tap_r[1]], axis=2), o_sp)
    h_sp[0] = o_sp[0]
    h_sp[1:, :, :block] = o_sp[1:, :, :block] - sign * o_sp[: seq_n - 1, :, block:]
    h_sp[1:, :, block:] = o_sp[1:, :, block:] + sign * o_sp[: seq_n - 1, :, :block]

    groups = half_n // group
    mine = me // half_n

    def send_back(q_sp, src, dst, slot, corr):
        for own in (False, True):
            half = mine if own else 1 - mine
            first = half * half_n
            block_conv(h_sp, q_sp, o_sp, block, group, corr, half * groups, groups)
            src[pl.ds(first, half_n)] = field(first, 1.0 / block).reshape(half_n, chans, block)
            half_exchange(src, dst, slot, half, own)

    send_back(x_sp, con_s, con_r, 3, False)
    arrived(dcn_r, 2)
    spectrum(dcn_r[...], d_sp)
    send_back(d_sp, dga_s, dga_r, 4, True)

    lanes = block // 4
    for half in (1, 0):
        first, end = half * half_n, (half + 1) * half_n
        block_conv(x_sp, d_sp, h_sp, block, group, True, half * groups, groups)
        if half:
            end = end - 1
            o_sp[end] = h_sp[end]
        o_sp[first:end, :, :block] = h_sp[first:end, :, :block] + sign * h_sp[first + 1 : end + 1, :, block:]
        o_sp[first:end, :, block:] = h_sp[first:end, :, block:] - sign * h_sp[first + 1 : end + 1, :, :block]
        term = field(first, scale / block)
        for r in range(4):
            gf_t[r] = term[:, r * lanes : (r + 1) * lanes]
            for d in range(dp_n):
                gf_s[half, d, :, r * lanes : (r + 1) * lanes] = gf_t[r, pl.ds(d, half_n, stride=chans), :]
        exchange(gf_s.at[half], gf_r.at[half], 5 + 9 * half, "dp")
    both = jnp.sum(gat_r[...] * dcn_r[...], axis=0)
    narrow = both[:, :lanes]
    for r in range(1, 4):
        narrow = narrow + both[:, r * lanes : (r + 1) * lanes]
    for d in range(dp_n):
        sk_s[d] = jnp.broadcast_to(narrow[d : d + 1, :], (8, lanes))
    exchange(sk_s, sk_r, 6, "dp")

    arrived(con_r, 3)
    gated = gat_s[...].reshape(width, block)
    conv = con_r[...].reshape(width, block) + skip_col * gated
    mixed = (conv * gate_out[...]).astype(BF16)
    dproj[pl.ds(0, width), :] = (dmx[...] * conv).astype(BF16)

    def fill(dst, first, term):
        term = term.reshape(seq_n // 2, 2, chans, width)
        for c in (0, 1):
            dst[c, :, :, first : first + width] = term[:, c]

    fill(g1_s, 0, dot(tok_t[...], dproj[pl.ds(0, width), :], NT))
    fill(g1_s, width, dot(mixed, cot[...]))
    swap(g1_s, p1_r, 7)
    out[...] = dot(mixed, w_o[...], TN).astype(BF16)
    arrived(p1_r, 7)
    r1_s[...] = g1_s[core] + p1_r[...]
    exchange(r1_s, r1_r, 12, cores=2)

    arrived(dga_r, 4)
    dgated = dga_r[...].reshape(width, block) + skip_col * dcn_s[...].reshape(width, block)
    dproj[pl.ds(width, width), :] = (dgated * values[...]).astype(BF16)
    dproj[pl.ds(2 * width, width), :] = (dgated * gate_in[...]).astype(BF16)
    for k in (0, 1):
        fill(g2_s, k * width, dot(tok_t[...], dproj[pl.ds((k + 1) * width, width), :], NT))
    swap(g2_s, p2_r, 9)
    arrived(p2_r, 9)
    r2_s[...] = g2_s[core] + p2_r[...]
    exchange(r2_s, r2_r, 13, cores=2)
    dinp[...] = dot(dproj[...], w_t[...], TN).astype(BF16)

    arrived(r1_r, 12)
    sum1 = jnp.sum(r1_r[...], axis=0) * scale
    piece = 2 * width // 4
    for r in range(4):
        z_s[:, r, :] = sum1[:, r * piece : (r + 1) * piece]
    arrived(r2_r, 13)
    sum2 = jnp.sum(r2_r[...], axis=0) * scale
    for r in range(4):
        z_s[:, 4 + r, :] = sum2[:, r * piece : (r + 1) * piece]
    exchange(z_s, z_r, 10, "dp")
    arrived(sk_r, 6)
    sk_sum = jnp.sum(sk_r[...], axis=0) * scale
    for half in (1, 0):
        arrived(gf_r.at[half], 5 + 9 * half)
        gf_sum = jnp.sum(gf_r[half], axis=0)
        for r in range(4):
            q_s[half * half_n : (half + 1) * half_n, r, :] = gf_sum[:, r * lanes : (r + 1) * lanes]
    q_s[:, 4, :] = jnp.broadcast_to(sk_sum[0:1, :], (seq_n, lanes))
    exchange(q_s, q_r, 8)

    arrived(z_r, 10)
    a_s[...] = jnp.sum(z_r[...], axis=0)
    exchange(a_s, a_r, 11, gather=True)
    arrived(q_r, 8)
    for r in range(4):
        gfil[:, r * lanes : (r + 1) * lanes] = q_r[:, r, :]
    gskip[...] = jnp.sum(q_r[:, 4, :].T, axis=0, keepdims=True)
    arrived(a_r, 11)

    def line(r):
        return jnp.concatenate([a_r[:, r, :], a_r[:, r + 1, :]], axis=1)

    gout[...] = line(2)
    for k, r in enumerate((0, 4, 6)):
        h, m, t = split3(line(r))
        gin[:, k * width : (k + 1) * width] = dot(h, perm) + (dot(m, perm) + dot(t, perm))

    for slot, ref in (
        (0, near),
        (1, gat_r),
        (2, dcn_r),
        (3, con_r),
        (4, dga_r),
        (5, gf_r.at[0]),
        (14, gf_r.at[1]),
        (6, sk_r),
        (8, q_r),
        (10, z_r),
        (11, a_r),
        (12, r1_r),
        (13, r2_r),
    ):
        sent(ref, slot)
    for slot, ref in ((7, p1_r), (9, p2_r), (15, near)):
        pltpu.make_async_copy(ref, ref, send.at[slot]).wait()


def deliver(*refs):
    half = len(refs) // 2
    for src, dst in zip(refs[:half], refs[half:]):
        dst[...] = src[...]


def shards(tokens, cotangent, w_in, w_out, filter_taps, skip):
    seq_n, dp_n = lax.axis_size("seq"), lax.axis_size("dp")
    block, width = tokens.shape[1:]
    chans = width // seq_n
    scale = 1.0 / math.sqrt(dp_n * seq_n * block)
    own = width // dp_n

    def shape(*dims, dtype=F32):
        return pltpu.VMEM(dims, dtype)

    ex = (seq_n, chans, block)
    sp = (seq_n, chans, 2 * block)
    scratch = [
        shape(2, seq_n, chans, block // 2),
        *[shape(*ex)] * 2,
        shape(2, seq_n, chans, block // 2),
        *[shape(*ex)] * 2,
        shape(3 * width, block),
        shape(width, block),
        shape(3 * width, width, dtype=BF16),
        shape(width, width, dtype=BF16),
        shape(width, block, dtype=BF16),
        shape(3 * block, 2 * block, dtype=BF16),
        shape(4 * block, block, dtype=BF16),
        *[shape(*sp)] * 4,
        *[shape(*ex)] * 4,
        shape(4, width // 2, block // 4),
        *[shape(2, dp_n, seq_n // 2, block)] * 2,
        *[shape(dp_n, 8, block // 4)] * 2,
        *[shape(seq_n, 8, block // 4)] * 2,
        shape(3 * width, block, dtype=BF16),
        *[shape(2, seq_n // 2, chans, 2 * width)] * 2,
        *[shape(seq_n // 2, chans, 2 * width)] * 6,
        *[shape(dp_n, 8, width // 2)] * 2,
        shape(8, width // 2),
        shape(seq_n, 8, width // 2),
        pltpu.SemaphoreType.DMA((16,)),
        pltpu.SemaphoreType.DMA((16,)),
    ]
    vmem = pl.BlockSpec(memory_space=pltpu.VMEM)
    anywhere = pl.BlockSpec(memory_space=pl.ANY)
    results = pl.pallas_call(
        functools.partial(body, seq_n, dp_n, scale),
        out_shape=(
            jax.ShapeDtypeStruct((block, width), BF16),
            jax.ShapeDtypeStruct((block, width), BF16),
            jax.ShapeDtypeStruct((own, 3 * width), F32),
            jax.ShapeDtypeStruct((own, width), F32),
            jax.ShapeDtypeStruct((own, block), F32),
            jax.ShapeDtypeStruct((1, own), F32),
        ),
        in_specs=[vmem] * 7,
        out_specs=(vmem,) * 6,
        scratch_shapes=scratch,
        compiler_params=pltpu.CompilerParams(
            collective_id=0, has_side_effects=True, vmem_limit_bytes=56 * 1024 * 1024
        ),
        name="operator",
    )(tokens[0], cotangent[0], w_in, w_out, filter_taps, skip[None], jnp.asarray(tables(block)))
    out, dinp, gin, gout, gfil, gskip = pl.pallas_call(
        deliver,
        out_shape=tuple(jax.ShapeDtypeStruct(r.shape, r.dtype) for r in results),
        in_specs=[vmem] * 6,
        out_specs=(vmem,) * 6,
        name="deliver",
    )(*results)
    return out[None], dinp[None], gin, gout, gfil.T, gskip[0]


def solution(mesh):
    return jax.shard_map(
        shards,
        mesh=mesh,
        in_specs=(P("dp", "seq", None), P("dp", "seq", None), P(), P(), P("seq", None), P()),
        out_specs=(
            P("dp", "seq", None),
            P("dp", "seq", None),
            P("dp", None),
            P("dp", None),
            P("seq", "dp"),
            P("dp"),
        ),
        check_vma=False,
    )
```

```python
import functools
import math

import jax
import jax.numpy as jnp
import numpy as np
from jax import lax
from jax.experimental import pallas as pl
from jax.experimental.pallas import tpu as pltpu
from jax.sharding import PartitionSpec as P

F32 = jnp.float32
BF16 = jnp.bfloat16
ROWS = 16
NT = (((1,), (1,)), ((), ()))
TN = (((0,), (0,)), ((), ()))


def tables(block):
    def turn(numer):
        angle = np.pi / (2 * block) * (numer % (4 * block))
        return np.cos(angle), np.sin(angle)

    pos = np.arange(block)
    coarse = np.arange(block // ROWS) * ROWS
    fine = np.arange(ROWS)
    odd = 2 * pos + 1
    parts = [
        *turn(np.outer(coarse, odd)),
        *turn(np.outer(fine, odd)),
        *turn(np.outer(2 * coarse, pos)),
        *turn(np.outer(2 * fine + 1, pos)),
    ]
    return np.concatenate(parts, axis=0).astype(np.float32)


def split2(x):
    high = x.astype(BF16)
    return high, (x - high.astype(F32)).astype(BF16)


def split3(x):
    high = x.astype(BF16)
    rest = x - high.astype(F32)
    mid = rest.astype(BF16)
    return high, mid, (rest - mid.astype(F32)).astype(BF16)


def dot(a, b, dims=(((1,), (0,)), ((), ()))):
    return lax.dot_general(a, b, dims, preferred_element_type=F32)


def block_conv(p_ref, q_ref, o_ref, block, size, corr, first, groups):
    total = q_ref.shape[0] // size
    lanes = min(128, block)

    def tile(t, _):
        re = pl.ds(pl.multiple_of(t * lanes, lanes), lanes)
        im = pl.ds(pl.multiple_of(block + t * lanes, lanes), lanes)

        def chunk(acc, out0, in0, diag):
            acc = list(acc)
            cache = {}
            base = in0 - out0 if corr else out0 - in0
            for u in range(size):
                qr, qi = q_ref[in0 + u, :, re], q_ref[in0 + u, :, im]
                qs = qr + qi
                for r in range(size):
                    lag = u - r if corr else r - u
                    if diag and lag < 0:
                        continue
                    if lag not in cache:
                        pr, pi = p_ref[base + lag, :, re], p_ref[base + lag, :, im]
                        both, diff = pr + pi, pi - pr
                        cache[lag] = (pr, -both, -diff) if corr else (pr, diff, both)
                    one, two, three = cache[lag]
                    acc[3 * r] = acc[3 * r] + one * qs
                    acc[3 * r + 1] = acc[3 * r + 1] + two * qr
                    acc[3 * r + 2] = acc[3 * r + 2] + three * qi
            return tuple(acc)

        def group(g, _):
            out0 = g * size
            zero = jnp.zeros((q_ref.shape[1], lanes), F32)
            acc = chunk((zero,) * (3 * size), out0, out0, True)

            def step(h, acc):
                return chunk(acc, out0, h * size, False)

            low, top = (g + 1, total) if corr else (0, g)
            acc = lax.fori_loop(low, top, step, acc)
            for r in range(size):
                o_ref[out0 + r, :, re] = acc[3 * r] - acc[3 * r + 2]
                o_ref[out0 + r, :, im] = acc[3 * r] + acc[3 * r + 1]
            return 0

        lax.fori_loop(first, first + groups, group, 0)
        return 0

    lax.fori_loop(0, block // lanes, tile, 0)


def farthest_first(step, mine, parts, ring):
    if ring:
        back = step % 2
        return (mine + back * (parts - (step + 1) // 2) + (1 - back) * (step // 2)) % parts

    def offset(i):
        return (i * (i + 1) // 2) % 4

    cores = parts // 16
    if cores == 0:
        return (mine + step) % parts
    chip = mine // cores
    x, y = chip // 4 + offset(step // (4 * cores)), chip % 4 + offset((step // cores) % 4)
    return ((x % 4) * 4 + y % 4) * cores + (mine + step) % cores


def body(
    seq_n,
    dp_n,
    scale,
    tok,
    cot,
    w_in,
    w_out,
    taps,
    skip,
    tab,
    out,
    dinp,
    gin,
    gout,
    gfil,
    gskip,
    tap_s,
    gat_s,
    dcn_s,
    tap_r,
    gat_r,
    dcn_r,
    proj,
    dmx,
    w_t,
    w_o,
    tok_t,
    f_mat,
    b_mat,
    h_sp,
    x_sp,
    d_sp,
    o_sp,
    con_s,
    dga_s,
    con_r,
    dga_r,
    gf_t,
    gf_s,
    gf_r,
    sk_s,
    sk_r,
    q_s,
    q_r,
    dproj,
    g1_s,
    g2_s,
    p1_r,
    p2_r,
    r1_s,
    r2_s,
    r1_r,
    r2_r,
    z_s,
    z_r,
    a_s,
    a_r,
    send,
    recv,
):
    block, width = tok.shape
    chans = width // seq_n
    me = lax.axis_index("seq")
    my_dp = lax.axis_index("dp")
    core = lax.rem(me, 2)
    group = 8 if seq_n >= 32 else 2

    barrier = pltpu.get_barrier_semaphore()

    def greet_seq(k, _):
        peer = farthest_first(seq_n - k, me, seq_n, False)
        pl.semaphore_signal(barrier, 1, device_id={"seq": peer})
        return 0

    def greet_dp(k, _):
        peer = farthest_first(dp_n - k, my_dp, dp_n, True)
        pl.semaphore_signal(barrier, 1, device_id={"dp": peer})
        return 0

    lax.fori_loop(1, seq_n, greet_seq, 0)
    lax.fori_loop(1, dp_n, greet_dp, 0)

    def exchange(src, dst, slot, axis="seq", gather=False, cores=1):
        mine, parts = (me // cores, seq_n // cores) if axis == "seq" else (my_dp, dp_n)
        own = src if gather else src.at[mine]
        pltpu.make_async_copy(own, dst.at[mine], recv.at[slot]).start()

        def go(k, _):
            peer = farthest_first(parts - k, mine, parts, axis == "dp")
            pltpu.make_async_remote_copy(
                src if gather else src.at[peer],
                dst.at[mine],
                send.at[slot],
                recv.at[slot],
                device_id={axis: peer if cores == 1 else peer * cores + core},
            ).start()
            return 0

        lax.fori_loop(1, parts, go, 0)

    half_n = seq_n // 2

    def half_exchange(src, dst, slot, half, own):
        if own:
            pltpu.make_async_copy(src.at[me], dst.at[me], recv.at[slot]).start()

        def go(k, _):
            step = half_n - 1 - k
            if half_n == 16:
                x, y = (me // 8 + step // 8) % 2, (me // 2 + (step // 2) * (step // 2 + 1) // 2) % 4
                peer = half * half_n + x * 8 + y * 2 + (me + step) % 2
            else:
                peer = half * half_n + (me + step) % half_n
            pltpu.make_async_remote_copy(
                src.at[peer],
                dst.at[me],
                send.at[slot],
                recv.at[slot],
                device_id={"seq": peer},
            ).start()
            return 0

        lax.fori_loop(0, half_n - 1 if own else half_n, go, 0)

    def swap(src, dst, slot):
        pltpu.make_async_remote_copy(
            src.at[1 - core],
            dst,
            send.at[slot],
            recv.at[slot],
            device_id={"seq": me + 1 - 2 * core},
        ).start()

    def arrived(dst, slot):
        pltpu.make_async_copy(dst, dst, recv.at[slot]).wait()

    def sent(dst, slot):
        rest = dst.at[pl.ds(0, dst.shape[0] - 1)]
        pltpu.make_async_copy(rest, rest, send.at[slot]).wait()

    row = lax.broadcasted_iota(jnp.int32, (width, width), 0)
    col = lax.broadcasted_iota(jnp.int32, (width, width), 1)
    hit = (col % seq_n) * chans + col // seq_n == row
    perm = jnp.where(hit, 1.0, 0.0).astype(BF16)

    high, low = split2(taps[...])
    taps_t = dot(perm, high, NT) + dot(perm, low, NT)
    for h in (0, 1):
        piece = taps_t[:, h * (block // 2) : (h + 1) * (block // 2)]
        tap_s[h] = piece.reshape(seq_n, chans, block // 2)
    pl.semaphore_wait(barrier, seq_n + dp_n - 2)

    parity = my_dp % 2
    near, far = tap_r.at[parity], tap_r.at[1 - parity]
    exchange(tap_s.at[parity], near, 0)
    for part in range(3):
        rows = pl.ds(part * width, width)
        w_t[rows, :] = dot(perm, w_in[:, part * width : (part + 1) * width], NT).astype(BF16)
    gate_out = proj.at[pl.ds(0, width)]
    gate_in = proj.at[pl.ds(width, width)]
    values = proj.at[pl.ds(2 * width, width)]
    gate_in[...] = dot(w_t[pl.ds(width, width), :], tok[...], NT)
    values[...] = dot(w_t[pl.ds(2 * width, width), :], tok[...], NT)
    gat_s[...] = (values[...] * gate_in[...]).reshape(seq_n, chans, block)
    exchange(gat_s, gat_r, 1)
    gate_out[...] = dot(w_t[pl.ds(0, width), :], tok[...], NT)
    w_o[...] = dot(perm, w_out[...]).astype(BF16)
    dmx[...] = dot(w_o[...], cot[...], NT)
    dcn_s[...] = (dmx[...] * gate_out[...]).reshape(seq_n, chans, block)
    exchange(dcn_s, dcn_r, 2)
    tok_t[...] = dot(perm, tok[...], NT).astype(BF16)
    skip_col = jnp.sum(jnp.where(hit, skip[...], 0.0), axis=1, keepdims=True)

    big = block // ROWS

    def build(dst, first, vertical):
        cos_f = tab[pl.ds(first + 2 * big, ROWS), :]
        sin_f = tab[pl.ds(first + 2 * big + ROWS, ROWS), :]

        def rows_of(a, _):
            cos_c = tab[pl.ds(first + a, 1), :]
            sin_c = tab[pl.ds(first + big + a, 1), :]
            cos = cos_c * cos_f - sin_c * sin_f
            sin = -(sin_c * cos_f + cos_c * sin_f)
            at = pl.multiple_of(a * ROWS, ROWS)
            for k, value in enumerate((cos, sin)):
                high, low = split2(value)
                for copy, piece in enumerate((high, low) if vertical else (high, high, low)):
                    if vertical:
                        dst[pl.ds((2 * copy + k) * block + at, ROWS), :] = piece
                    else:
                        dst[pl.ds(copy * block + at, ROWS), k * block : (k + 1) * block] = piece
            return 0

        lax.fori_loop(0, big, rows_of, 0)

    build(f_mat, 0, False)
    arrived(near, 0)
    for low, side in ((0, 1), (half_n, dp_n - 1)):
        piece = near.at[pl.ds(low, half_n)]
        pltpu.make_async_remote_copy(
            piece, piece, send.at[15], recv.at[15], device_id={"dp": (my_dp + side) % dp_n}
        ).start()
    build(b_mat, 2 * big + 2 * ROWS, True)

    rows_n = seq_n * chans
    step = min(256, block)

    def spectrum(src, dst):
        high, low = split2(src.reshape(rows_n, block))
        wide = jnp.concatenate([high, low, high], axis=1)
        for n in range(0, 2 * block, step):
            dst[:, :, n : n + step] = dot(wide, f_mat[:, n : n + step]).reshape(seq_n, chans, step)

    def field(first, factor):
        rows = half_n * chans
        high, low = split2(o_sp[pl.ds(first, half_n)].reshape(rows, 2 * block))
        wide = dot(jnp.concatenate([high, low], axis=0), b_mat[: 2 * block, :])
        return (wide[:rows] + wide[rows:] + dot(high, b_mat[2 * block :, :])) * factor

    odd = lax.broadcasted_iota(jnp.int32, (1, 1, block), 2) % 2
    sign = (1 - 2 * odd).astype(F32)

    arrived(gat_r, 1)
    spectrum(gat_r[...], x_sp)
    arrived(far, 15)
    spectrum(jnp.concatenate([tap_r[0], tap_r[1]], axis=2), o_sp)
    h_sp[0] = o_sp[0]
    h_sp[1:, :, :block] = o_sp[1:, :, :block] - sign * o_sp[: seq_n - 1, :, block:]
    h_sp[1:, :, block:] = o_sp[1:, :, block:] + sign * o_sp[: seq_n - 1, :, :block]

    groups = half_n // group
    mine = me // half_n

    def send_back(q_sp, src, dst, slot, corr):
        for own in (False, True):
            half = mine if own else 1 - mine
            first = half * half_n
            block_conv(h_sp, q_sp, o_sp, block, group, corr, half * groups, groups)
            src[pl.ds(first, half_n)] = field(first, 1.0 / block).reshape(half_n, chans, block)
            half_exchange(src, dst, slot, half, own)

    send_back(x_sp, con_s, con_r, 3, False)
    arrived(dcn_r, 2)
    spectrum(dcn_r[...], d_sp)
    send_back(d_sp, dga_s, dga_r, 4, True)

    lanes = block // 4
    for half in (1, 0):
        first, end = half * half_n, (half + 1) * half_n
        block_conv(x_sp, d_sp, h_sp, block, group, True, half * groups, groups)
        if half:
            end = end - 1
            o_sp[end] = h_sp[end]
        o_sp[first:end, :, :block] = h_sp[first:end, :, :block] + sign * h_sp[first + 1 : end + 1, :, block:]
        o_sp[first:end, :, block:] = h_sp[first:end, :, block:] - sign * h_sp[first + 1 : end + 1, :, :block]
        term = field(first, scale / block)
        for r in range(4):
            gf_t[r] = term[:, r * lanes : (r + 1) * lanes]
            for d in range(dp_n):
                gf_s[half, d, :, r * lanes : (r + 1) * lanes] = gf_t[r, pl.ds(d, half_n, stride=chans), :]
        exchange(gf_s.at[half], gf_r.at[half], 5 + 9 * half, "dp")
    arrived(con_r, 3)
    gated = gat_s[...].reshape(width, block)
    conv = con_r[...].reshape(width, block) + skip_col * gated
    mixed = (conv * gate_out[...]).astype(BF16)
    dproj[pl.ds(0, width), :] = (dmx[...] * conv).astype(BF16)

    def fill(dst, first, term):
        term = term.reshape(seq_n // 2, 2, chans, width)
        for c in (0, 1):
            dst[c, :, :, first : first + width] = term[:, c]

    fill(g1_s, 0, dot(tok_t[...], dproj[pl.ds(0, width), :], NT))
    fill(g1_s, width, dot(mixed, cot[...]))
    swap(g1_s, p1_r, 7)
    both = jnp.sum(gat_r[...] * dcn_r[...], axis=0)
    narrow = both[:, :lanes]
    for r in range(1, 4):
        narrow = narrow + both[:, r * lanes : (r + 1) * lanes]
    for d in range(dp_n):
        sk_s[d] = jnp.broadcast_to(narrow[d : d + 1, :], (8, lanes))
    exchange(sk_s, sk_r, 6, "dp")
    arrived(p1_r, 7)
    r1_s[...] = g1_s[core] + p1_r[...]
    exchange(r1_s, r1_r, 12, cores=2)

    arrived(dga_r, 4)
    dgated = dga_r[...].reshape(width, block) + skip_col * dcn_s[...].reshape(width, block)
    dproj[pl.ds(width, width), :] = (dgated * values[...]).astype(BF16)
    dproj[pl.ds(2 * width, width), :] = (dgated * gate_in[...]).astype(BF16)
    for k in (0, 1):
        fill(g2_s, k * width, dot(tok_t[...], dproj[pl.ds((k + 1) * width, width), :], NT))
    swap(g2_s, p2_r, 9)
    arrived(p2_r, 9)
    r2_s[...] = g2_s[core] + p2_r[...]
    exchange(r2_s, r2_r, 13, cores=2)
    out[...] = dot(mixed, w_o[...], TN).astype(BF16)
    dinp[...] = dot(dproj[...], w_t[...], TN).astype(BF16)

    arrived(r1_r, 12)
    sum1 = jnp.sum(r1_r[...], axis=0) * scale
    piece = 2 * width // 4
    for r in range(4):
        z_s[:, r, :] = sum1[:, r * piece : (r + 1) * piece]
    arrived(r2_r, 13)
    sum2 = jnp.sum(r2_r[...], axis=0) * scale
    for r in range(4):
        z_s[:, 4 + r, :] = sum2[:, r * piece : (r + 1) * piece]
    exchange(z_s, z_r, 10, "dp")
    arrived(sk_r, 6)
    sk_sum = jnp.sum(sk_r[...], axis=0) * scale
    for half in (1, 0):
        arrived(gf_r.at[half], 5 + 9 * half)
        gf_sum = jnp.sum(gf_r[half], axis=0)
        for r in range(4):
            q_s[half * half_n : (half + 1) * half_n, r, :] = gf_sum[:, r * lanes : (r + 1) * lanes]
    q_s[:, 4, :] = jnp.broadcast_to(sk_sum[0:1, :], (seq_n, lanes))
    exchange(q_s, q_r, 8)

    arrived(z_r, 10)
    a_s[...] = jnp.sum(z_r[...], axis=0)
    exchange(a_s, a_r, 11, gather=True)
    arrived(q_r, 8)
    for r in range(4):
        gfil[:, r * lanes : (r + 1) * lanes] = q_r[:, r, :]
    gskip[...] = jnp.sum(q_r[:, 4, :].T, axis=0, keepdims=True)
    arrived(a_r, 11)

    def line(r):
        return jnp.concatenate([a_r[:, r, :], a_r[:, r + 1, :]], axis=1)

    gout[...] = line(2)
    for k, r in enumerate((0, 4, 6)):
        h, m, t = split3(line(r))
        gin[:, k * width : (k + 1) * width] = dot(h, perm) + (dot(m, perm) + dot(t, perm))

    for slot, ref in (
        (0, near),
        (1, gat_r),
        (2, dcn_r),
        (3, con_r),
        (4, dga_r),
        (5, gf_r.at[0]),
        (14, gf_r.at[1]),
        (6, sk_r),
        (8, q_r),
        (10, z_r),
        (11, a_r),
        (12, r1_r),
        (13, r2_r),
    ):
        sent(ref, slot)
    for slot, ref in ((7, p1_r), (9, p2_r), (15, near)):
        pltpu.make_async_copy(ref, ref, send.at[slot]).wait()


def deliver(*refs):
    half = len(refs) // 2
    for src, dst in zip(refs[:half], refs[half:]):
        dst[...] = src[...]


def shards(tokens, cotangent, w_in, w_out, filter_taps, skip):
    seq_n, dp_n = lax.axis_size("seq"), lax.axis_size("dp")
    block, width = tokens.shape[1:]
    chans = width // seq_n
    scale = 1.0 / math.sqrt(dp_n * seq_n * block)
    own = width // dp_n

    def shape(*dims, dtype=F32):
        return pltpu.VMEM(dims, dtype)

    ex = (seq_n, chans, block)
    sp = (seq_n, chans, 2 * block)
    scratch = [
        shape(2, seq_n, chans, block // 2),
        *[shape(*ex)] * 2,
        shape(2, seq_n, chans, block // 2),
        *[shape(*ex)] * 2,
        shape(3 * width, block),
        shape(width, block),
        shape(3 * width, width, dtype=BF16),
        shape(width, width, dtype=BF16),
        shape(width, block, dtype=BF16),
        shape(3 * block, 2 * block, dtype=BF16),
        shape(4 * block, block, dtype=BF16),
        *[shape(*sp)] * 4,
        *[shape(*ex)] * 4,
        shape(4, width // 2, block // 4),
        *[shape(2, dp_n, seq_n // 2, block)] * 2,
        *[shape(dp_n, 8, block // 4)] * 2,
        *[shape(seq_n, 8, block // 4)] * 2,
        shape(3 * width, block, dtype=BF16),
        *[shape(2, seq_n // 2, chans, 2 * width)] * 2,
        *[shape(seq_n // 2, chans, 2 * width)] * 6,
        *[shape(dp_n, 8, width // 2)] * 2,
        shape(8, width // 2),
        shape(seq_n, 8, width // 2),
        pltpu.SemaphoreType.DMA((16,)),
        pltpu.SemaphoreType.DMA((16,)),
    ]
    vmem = pl.BlockSpec(memory_space=pltpu.VMEM)
    anywhere = pl.BlockSpec(memory_space=pl.ANY)
    results = pl.pallas_call(
        functools.partial(body, seq_n, dp_n, scale),
        out_shape=(
            jax.ShapeDtypeStruct((block, width), BF16),
            jax.ShapeDtypeStruct((block, width), BF16),
            jax.ShapeDtypeStruct((own, 3 * width), F32),
            jax.ShapeDtypeStruct((own, width), F32),
            jax.ShapeDtypeStruct((own, block), F32),
            jax.ShapeDtypeStruct((1, own), F32),
        ),
        in_specs=[vmem] * 7,
        out_specs=(vmem,) * 6,
        scratch_shapes=scratch,
        compiler_params=pltpu.CompilerParams(
            collective_id=0, has_side_effects=True, vmem_limit_bytes=56 * 1024 * 1024
        ),
        name="operator",
    )(tokens[0], cotangent[0], w_in, w_out, filter_taps, skip[None], jnp.asarray(tables(block)))
    out, dinp, gin, gout, gfil, gskip = pl.pallas_call(
        deliver,
        out_shape=tuple(jax.ShapeDtypeStruct(r.shape, r.dtype) for r in results),
        in_specs=[vmem] * 6,
        out_specs=(vmem,) * 6,
        name="deliver",
    )(*results)
    return out[None], dinp[None], gin, gout, gfil.T, gskip[0]


def solution(mesh):
    return jax.shard_map(
        shards,
        mesh=mesh,
        in_specs=(P("dp", "seq", None), P("dp", "seq", None), P(), P(), P("seq", None), P()),
        out_specs=(
            P("dp", "seq", None),
            P("dp", "seq", None),
            P("dp", None),
            P("dp", None),
            P("seq", "dp"),
            P("dp"),
        ),
        check_vma=False,
    )
```
